512 devices in a mesh: seq: 64 (over z, y), exp: 8 (over x, core).
Axes of the slice: x: 4, y: 4, z: 16, core: 2. Of those that a mesh axis runs over, the one named last changes fastest.
Arguments:
- x_in: bfloat16 [4096, 8192], P('seq', 'exp'), may hold values from -6 to 6
- z_gate: bfloat16 [4096, 8192], P('seq', 'exp'), may hold values from -6 to 6
- dt_low: bfloat16 [4096, 256], P('seq'), may hold values from -6 to 6
- dt_weight: bfloat16 [256, 8192], P(None, 'exp'), may hold values from -0.375 to 0.375
- dt_bias: float32 [8192], P('exp'), may hold values from -9 to -1
- a_log: float32 [16, 8192], P(None, 'exp'), may hold values from -4 to 0
- conv_weight: float32 [4, 8192], P(None, 'exp'), may hold values from -3 to 3
- conv_bias: float32 [8192], P('exp'), may hold values from -0.5 to 0.5
- d_skip: float32 [8192], P('exp'), may hold values from 0.5 to 1.5
- b_and_c: float32 [2, 16, 4096], P(None, None, 'seq'), may hold values from -6 to 6
- hidden: bfloat16 [4096, 4096], P('seq', 'exp'), may hold values from -6 to 6
- router: bfloat16 [4096, 8], P('exp'), may hold values from -0.09375 to 0.09375
- expert_ids: int32 [4096, 2], P('seq'), may hold values from 0 to 7, all different within a row; in each aligned block of 64 rows (0 to 63, 64 to 127, ...) at most 18 rows name the same one
- w_gate: bfloat16 [4096, 98304], P('exp', 'seq'), may hold values from -0.09375 to 0.09375
- w_down: bfloat16 [98304, 4096], P('seq', 'exp'), may hold values from -0.0546875 to 0.0546875
Outputs:
- mamba_out: bfloat16 [4096, 8192], P('seq', 'exp')
- moe_out: bfloat16 [4096, 4096], P('seq', 'exp')
The draws below stay inside these ranges and needn't reach their ends.
Inputs may be any that keep to these rules, and one draw needn't show every extreme that they name: `expert_ids`: each token names 2 different experts; among the 64 tokens of one block no expert is named more than 18 times, a bound that some expert reaches in every block.
All inputs are finite; a program needn't handle non-finite values.
Results may differ from the reference program's by a relative error of at most 0.018.
Values may be sent and summed in bfloat16 or wider, within the bound.
A program may use at most 128 MiB of HBM per device.

```python
import math
import jax
import jax.numpy as jnp
import numpy as np
from jax import lax

D = 4096
INNER = 8192
STATE = 16
CONV = 4
RANK = 256
EXPERTS = 8
TOPK = 2
FF = 12288
TOK_DEV = 64
CAP = 18
TOKENS = 4096
N_SEQ = 64
N_EXP = 8


def levels(own_key, dims, pieces, low, high):
    gain = 1.0
    for axis_at, blocks in pieces:
        draws = jax.random.uniform(jax.random.fold_in(jax.random.fold_in(own_key, 6), axis_at), (blocks,), jnp.float32, low / len(pieces), high / len(pieces))
        gain = gain * jnp.repeat(jnp.exp(draws), dims[axis_at] // blocks).reshape((-1,) + (1,) * (len(dims) - 1 - axis_at))
    return gain


def shared_out(stream_key, own, number, rows, amount, top, reach, skew):
    ranking = jax.random.permutation(stream_key, amount)
    crowded, common = portions_of(amount, rows * top, reach, skew, True), portions_of(amount, rows * top, reach, skew, False)
    places = jnp.arange(amount)

    def named(sizes, offset_by):
        used = int((sizes > 0).sum())
        fixed = max(1, used // 4)
        moved = fixed + (places - fixed + offset_by * (used - fixed)) % max(1, amount - fixed)
        return jnp.zeros((amount,), jnp.int32).at[ranking[jnp.where(places < fixed, places, moved)]].set(jnp.asarray(sizes, jnp.int32))

    sizes = jnp.where(number % 4 == 0, named(crowded, number // 4), named(common, number - number // 4 - 1))
    mixed = jax.random.permutation(jax.random.fold_in(own, 3), amount)
    donor, sink = mixed[0:amount // 2 * 2:2], mixed[1:amount // 2 * 2:2]
    room = jnp.minimum(sizes[donor] - 1, reach - sizes[sink]) // 2
    room = jnp.where((donor == ranking[0]) | (sink == ranking[0]) | (sizes[sink] == 0), 0, jnp.maximum(room, 0))
    moved = jax.random.randint(jax.random.fold_in(own, 4), (amount // 2,), 0, 1 << 20) % (room + 1)
    sizes = sizes.at[donor].add(-moved).at[sink].add(moved)
    labels = jnp.searchsorted(jnp.cumsum(sizes), jnp.arange(rows * top), side="right").astype(jnp.int32)
    table = labels.reshape(top, rows).T
    table = table[jax.random.permutation(jax.random.fold_in(own, 1), rows)]
    offset_by = jax.random.randint(jax.random.fold_in(own, 2), (rows, 1), 0, top)
    return jnp.take_along_axis(table, (jnp.arange(top)[None, :] + offset_by) % top, axis=1)


def portions_of(number_of, total, reach, slope, full):
    loads = [(1 << 20) // math.isqrt(grade ** slope) + 1 for grade in range(1, number_of + 1)]
    largest = reach if full else min(reach, max(-(-total // number_of), total * loads[0] // sum(loads)))
    least = 1 if total - largest >= number_of - 1 else 0
    holding, spare = [largest] + [least] * (number_of - 1), total - largest - least * (number_of - 1)
    while spare > 0:
        movable = [i for i in range(1, number_of) if holding[i] < largest] or [i for i in range(1, number_of) if holding[i] < reach]
        mass, budget = sum([loads[i] for i in movable]), spare
        for i in movable:
            extra = min(reach - holding[i], max(1, budget * loads[i] // mass), spare)
            holding[i] = holding[i] + extra
            spare = spare - extra
    return np.array(holding)


def gaussian(rng, shape, deviation, reach, shards=(), kind=jnp.bfloat16):
    result = deviation * jax.random.normal(rng, shape, jnp.float32)
    if shards:
        result = result * levels(rng, shape, shards, -0.22, 0.18)
    return jnp.clip(result, -reach, reach).astype(kind)


def setup_inputs(seed: int = 0) -> dict:
    key_of = jax.random.split(jax.random.key(seed), 16)
    x_in = gaussian(key_of[0], (TOKENS, INNER), 1.0, 6.0, ((0, 64), (1, 8)))
    z_gate = gaussian(key_of[1], (TOKENS, INNER), 1.0, 6.0, ((0, 64), (1, 8)))
    dt_low = gaussian(key_of[2], (TOKENS, RANK), 1.0, 6.0, ((0, 64),))
    dt_weight = gaussian(key_of[3], (RANK, INNER), RANK ** -0.5, 0.375, ((1, 8),))
    dt_bias = jnp.clip(-9.0 + 8.0 * jax.random.uniform(key_of[4], (INNER,), jnp.float32) ** levels(key_of[4], (INNER,), ((0, 8),), -0.2, 0.2), -9.0, -1.0)
    a_log = jnp.clip(-4.0 + 4.0 * jax.random.uniform(key_of[5], (STATE, INNER), jnp.float32) ** levels(key_of[5], (STATE, INNER), ((1, 8),), -0.2, 0.2), -4.0, 0.0)
    conv_weight = gaussian(key_of[6], (CONV, INNER), CONV ** -0.5, 3.0, ((1, 8),), jnp.float32)
    conv_bias = jnp.clip(jax.random.uniform(key_of[7], (INNER,), jnp.float32, -0.5, 0.5) * levels(key_of[7], (INNER,), ((0, 8),), -0.4, 0.0), -0.5, 0.5)
    d_skip = jnp.clip(0.5 + 1.0 * jax.random.uniform(key_of[8], (INNER,), jnp.float32) ** levels(key_of[8], (INNER,), ((0, 8),), -0.2, 0.2), 0.5, 1.5)
    b_and_c = gaussian(key_of[9], (2, STATE, TOKENS), 1.0, 6.0, ((2, 64),), jnp.float32)
    hidden = gaussian(key_of[10], (TOKENS, D), 1.0, 6.0, ((0, 64), (1, 8)))
    router = gaussian(key_of[11], (D, EXPERTS), D ** -0.5, 0.09375, ((0, 8),))
    expert_ids_keys = jax.random.split(jax.random.fold_in(key_of[12], 1), TOKENS // TOK_DEV)
    expert_ids_turns = jax.random.permutation(jax.random.fold_in(key_of[12], 3), TOKENS // TOK_DEV)
    expert_ids = jax.vmap(lambda own, number: shared_out(jax.random.fold_in(key_of[12], 2), own, number, TOK_DEV, EXPERTS, TOPK, CAP, 2))(expert_ids_keys, expert_ids_turns).reshape((TOKENS, TOPK))
    w_gate = gaussian(key_of[13], (D, EXPERTS * FF), D ** -0.5, 0.09375, ((0, 8), (1, 64)))
    w_down = gaussian(key_of[14], (EXPERTS * FF, D), FF ** -0.5, 0.0546875, ((0, 64), (1, 8)))
    return dict(x_in=x_in, z_gate=z_gate, dt_low=dt_low, dt_weight=dt_weight, dt_bias=dt_bias, a_log=a_log, conv_weight=conv_weight, conv_bias=conv_bias, d_skip=d_skip, b_and_c=b_and_c, hidden=hidden, router=router, expert_ids=expert_ids, w_gate=w_gate, w_down=w_down)


def reference(x_in, z_gate, dt_low, dt_weight, dt_bias, a_log, conv_weight, conv_bias, d_skip, b_and_c, hidden, router, expert_ids, w_gate, w_down):
    padded = jnp.concatenate([jnp.zeros((CONV - 1, INNER), jnp.float32), x_in.astype(jnp.float32)], axis=0)
    convolved = jnp.zeros((TOKENS, INNER), jnp.float32) + conv_bias[None, :]
    for offset in range(CONV):
        convolved = convolved + conv_weight[offset][None, :] * padded[offset:offset + TOKENS]
    activated = jax.nn.silu(convolved)
    delta = jax.nn.softplus(jnp.dot(dt_low, dt_weight, preferred_element_type=jnp.float32) + dt_bias[None, :])
    rates = -jnp.exp(a_log)

    def advance(state, inputs):
        step_delta, step_x, step_b, step_c = inputs
        state = jnp.exp(step_delta[None, :] * rates) * state + step_b[:, None] * (step_delta * step_x)[None, :]
        return state, jnp.sum(step_c[:, None] * state, axis=0)

    start_state = jnp.zeros((STATE, INNER), jnp.float32)
    final_state, readout = lax.scan(advance, start_state, (delta, activated, b_and_c[0].T, b_and_c[1].T))
    mamba_out = ((readout + d_skip[None, :] * activated) * jax.nn.silu(z_gate.astype(jnp.float32))).astype(jnp.bfloat16)

    logits = jnp.dot(hidden, router, preferred_element_type=jnp.float32)
    picked = jnp.take_along_axis(logits, expert_ids, axis=1)
    gates = jax.nn.sigmoid(picked - picked[:, ::-1])
    blocks = expert_ids.reshape(N_SEQ, TOK_DEV * TOPK)
    onehot = (blocks[:, :, None] == jnp.arange(EXPERTS, dtype=jnp.int32)[None, None, :]).astype(jnp.int32)
    before = (jnp.cumsum(onehot, axis=1) - onehot).astype(jnp.int32)
    slots = jnp.sum(before * onehot, axis=2).astype(jnp.int32).reshape(TOKENS, TOPK)
    block_of = (jnp.arange(TOKENS, dtype=jnp.int32) // TOK_DEV)[:, None]
    rows_at = (block_of * CAP + slots).astype(jnp.int32)
    token_index = jnp.broadcast_to(jnp.arange(TOKENS, dtype=jnp.int32)[:, None], (TOKENS, TOPK))
    table = jnp.zeros((EXPERTS, N_SEQ * CAP), jnp.int32).at[expert_ids.reshape(-1), rows_at.reshape(-1)].set(token_index.reshape(-1))
    filled = jnp.zeros((EXPERTS, N_SEQ * CAP), jnp.bool_).at[expert_ids.reshape(-1), rows_at.reshape(-1)].set(True)
    slice_width = D // N_EXP

    def one_expert(index):
        routed = jnp.where(filled[index][:, None], hidden[table[index]], jnp.zeros((), jnp.bfloat16))
        gate_cols = lax.dynamic_slice_in_dim(w_gate, index * FF, FF, 1)
        split_in = routed.astype(jnp.float32).reshape(N_SEQ * CAP, N_EXP, slice_width)
        split_w = gate_cols.astype(jnp.float32).reshape(N_EXP, slice_width, FF)
        parts = jnp.einsum("rqd,qdf->rqf", split_in, split_w).astype(jnp.bfloat16)
        parts = lax.optimization_barrier(parts).astype(jnp.float32)
        acted = jax.nn.silu(jnp.sum(parts, axis=1)).astype(jnp.bfloat16)
        down_rows = lax.dynamic_slice_in_dim(w_down, index * FF, FF, 0)
        return jnp.dot(acted.astype(jnp.float32), down_rows.astype(jnp.float32), preferred_element_type=jnp.float32)

    expert_out = lax.map(one_expert, jnp.arange(EXPERTS, dtype=jnp.int32))
    chosen = expert_out[expert_ids, rows_at]
    moe_out = jnp.sum(gates[:, :, None] * chosen, axis=1).astype(jnp.bfloat16)
    return mamba_out, moe_out
```

```python
import functools

import jax
import jax.numpy as jnp
from jax import lax
from jax.experimental import pallas as pl
from jax.experimental.pallas import tpu as pltpu
from jax.sharding import PartitionSpec as P

CAP = 18
PAD = 32
NZ, NY, NX = 16, 4, 4
MESH = pl.DeviceIdType.MESH
BF, F32 = jnp.bfloat16, jnp.float32
BATCHES = 4


def dot(a, b):
    return jnp.dot(a, b, preferred_element_type=F32)


class Mail:
    def __init__(self, send, recv):
        self.send, self.recv, self.count, self.sent = send, recv, 0, []

    def post(self, src, dst, slot, to, unless=None):
        copy = pltpu.make_async_remote_copy(
            src_ref=src, dst_ref=dst, send_sem=self.send.at[self.count], recv_sem=self.recv.at[slot],
            device_id=to, device_id_type=MESH)
        self.count += 1
        self.sent.append((copy, unless))
        if unless is None:
            copy.start()
        else:
            pl.when(jnp.logical_not(unless))(copy.start)

    def take(self, dst, slot, unless=None):
        copy = pltpu.make_async_remote_copy(
            src_ref=dst, dst_ref=dst, send_sem=self.send.at[0], recv_sem=self.recv.at[slot],
            device_id=(lax.axis_index("seq"), lax.axis_index("exp")), device_id_type=MESH)
        if unless is None:
            copy.wait_recv()
        else:
            pl.when(jnp.logical_not(unless))(copy.wait_recv)

    def finish(self):
        for copy, unless in self.sent:
            if unless is None:
                copy.wait_send()
            else:
                pl.when(jnp.logical_not(unless))(copy.wait_send)


def expert_kernel(hid, router_t, ids_t, wg_in, wd_in, out,
                  wg, wd, pack, in1, rt, sbuf, rbuf, act, prod, ys, yc, zs, zr, back, ret, lgs, lgr,
                  send, recv, local):
    seq, exp = lax.axis_index("seq"), lax.axis_index("exp")
    z, y, x, c = seq // NY, lax.rem(seq, NY), exp // 2, lax.rem(exp, 2)
    half = lax.rem(z, 2)
    zpair = z + 1 - 2 * half
    near = {1: lax.rem(y + 1, NY), -1: lax.rem(y + NY - 1, NY)}
    xs = {d: lax.rem(x + d + NX, NX) for d in (-1, 0, 1, 2)}
    ff = wg.shape[3]

    def at(z_, y_, x_, c_):
        return (z_ * NY + y_, x_ * 2 + c_)

    mate = at(z, y, x, 1 - c)
    ypeer = {d: at(z, near[d], x, c) for d in (1, -1)}
    xpeer = {d: at(z, y, xs[d], c) for d in (1, -1)}
    zpeer = at(zpair, y, x, c)
    experts = 8

    barrier = pltpu.get_barrier_semaphore()
    home = half == c

    def greet(to):
        pl.semaphore_signal(barrier, inc=1, device_id=to, device_id_type=MESH)

    order = [4, 3, 5, 2, 6, 1, 7, 0]
    groups = [lax.rem(z // 2 + off, experts) for off in order]
    for e, off in zip(groups, order):
        to = at(2 * e + c, y, x, half)
        if off == 0:
            pl.when(jnp.logical_not(home))(functools.partial(greet, to))
        else:
            greet(to)
    for to in (zpeer, ypeer[1], ypeer[-1]):
        greet(to)
    for j in range(1, 8):
        greet((seq, lax.rem(exp + j, 8)))

    loads = []
    for q in range(NX):
        loads.append(pltpu.make_async_copy(wg_in.at[:, pl.ds(q * ff, ff)], wg.at[c, q], local.at[q]))
    loads.append(pltpu.make_async_copy(wd_in, wd.at[c], local.at[NX]))
    for copy in loads:
        copy.start()

    ids = ids_t[...]
    tokens = ids.shape[1]
    e_iota = lax.broadcasted_iota(jnp.int32, (experts, tokens), 0)
    hits = [(ids[k:k + 1, :] == e_iota).astype(F32) for k in range(2)]
    ahead = (lax.broadcasted_iota(jnp.int32, (tokens, tokens), 0)
             < lax.broadcasted_iota(jnp.int32, (tokens, tokens), 1)).astype(BF)
    before = dot((hits[0] + hits[1]).astype(BF), ahead)
    keys = [ids[k:k + 1, :] * PAD + jnp.sum(hits[k] * before, axis=0, keepdims=True).astype(jnp.int32)
            for k in range(2)]
    r_iota = lax.broadcasted_iota(jnp.int32, (experts * PAD, tokens), 0)
    match = [r_iota == keys[k] for k in range(2)]
    selector = jnp.where(match[0] | match[1], 1.0, 0.0).astype(BF)
    h = hid[...]
    pack[...] = dot(selector, h).astype(BF).reshape(pack.shape)
    lg = lax.dot_general(router_t[...], h, (((1,), (1,)), ((), ())), preferred_element_type=F32)
    lgs[...] = jnp.concatenate([lg, jnp.zeros((experts, 128 - tokens), F32)], axis=1)
    rows = CAP * experts
    r_c = lax.broadcasted_iota(jnp.int32, (rows, experts * PAD), 0)
    q_c = lax.broadcasted_iota(jnp.int32, (rows, experts * PAD), 1)
    group = sum((r_c >= CAP * m).astype(jnp.int32) for m in range(1, experts))
    tight = jnp.where(q_c == r_c + (PAD - CAP) * group, 1.0, 0.0).astype(BF)
    q_e = lax.broadcasted_iota(jnp.int32, (experts * PAD, rows), 0)
    r_e = lax.broadcasted_iota(jnp.int32, (experts * PAD, rows), 1)
    group_e = sum((r_e >= CAP * m).astype(jnp.int32) for m in range(1, experts))
    loose = jnp.where(q_e == r_e + (PAD - CAP) * group_e, 1.0, 0.0).astype(BF)

    mail = Mail(send, recv)
    pl.semaphore_wait(barrier, 8 + 3 + 7 - home.astype(jnp.int32))

    IN1, RT, RS, ACT = 0, 8, 16, 28
    YS, YC, ZR, RET, LG, WG, WD = 44, 46, 48, 49, 57, 65, 69

    for e, off in zip(groups, order):
        mail.post(pack.at[e], in1.at[z // 2], IN1 + z // 2, at(2 * e + c, y, x, half),
                  home if off == 0 else None)
    own_group = z // 2
    stay = pltpu.make_async_copy(pack.at[own_group], in1.at[own_group], local.at[NX + 1])
    pl.when(home)(stay.start)
    for q in range(NX):
        mail.post(wg_in.at[:, pl.ds(q * ff, ff)], wg.at[c, q], WG + q, mate)
    mail.post(wd_in, wd.at[c], WD, mate)
    for j in range(1, 8):
        mail.post(lgs, lgr.at[exp], LG + exp, (seq, lax.rem(exp + j, 8)))
    pl.when(home)(stay.wait)
    for e, off in zip(groups, order):
        mail.take(in1.at[e], IN1 + e, home if off == 0 else None)

    rt[0, half] = dot(tight, in1[...].reshape(experts * PAD, -1)).astype(BF)
    other = 1 - half
    mail.post(rt.at[0, half], rt.at[0, half], RT + half, zpeer)
    mail.post(rt.at[0, half], rt.at[2, half], RT + 4 + half, ypeer[1])
    mail.post(rt.at[0, half], rt.at[1, half], RT + 2 + half, ypeer[-1])
    mail.take(rt.at[0, other], RT + other)
    mail.post(rt.at[0, other], rt.at[2, other], RT + 4 + other, ypeer[1])
    mail.post(rt.at[0, other], rt.at[1, other], RT + 2 + other, ypeer[-1])
    for copy in loads:
        copy.wait()
    for q in range(NX):
        mail.take(wg.at[1 - c, q], WG + q)

    def gathered(k):
        if k == 1:
            mail.take(rt.at[1, 1], RT + 3)
            mail.post(rt.at[1, 1], rt.at[3, 1], RT + 7, ypeer[-1])
            mail.take(rt.at[1, 0], RT + 2)
        elif k == 2:
            mail.take(rt.at[2, 0], RT + 4)
            mail.post(rt.at[2, 0], rt.at[3, 0], RT + 6, ypeer[1])
            mail.take(rt.at[2, 1], RT + 5)
        elif k == 3:
            mail.take(rt.at[3, 0], RT + 6)
            mail.take(rt.at[3, 1], RT + 7)

    def part(k, q):
        return dot(rt[k, 0], wg[0, q]) + dot(rt[k, 1], wg[1, q])

    way = [1 if k % 2 == 0 else -1 for k in range(BATCHES)]
    kept = {}

    def first(k):
        d = way[k]
        sbuf[k, 0] = part(k, xs[2]).astype(BF)
        mail.post(sbuf.at[k, 0], rbuf.at[k, 0], RS + 3 * k, xpeer[d])
        sbuf[k, 1] = part(k, xs[-d]).astype(BF)
        mail.post(sbuf.at[k, 1], rbuf.at[k, 1], RS + 3 * k + 1, xpeer[-d])
        sbuf[k, 2] = part(k, xs[d]).astype(BF)
        sbuf[k, 3] = part(k, x).astype(BF)

    def second(k):
        d = way[k]
        mail.take(rbuf.at[k, 0], RS + 3 * k)
        sbuf[k, 4] = (sbuf[k, 2].astype(F32) + rbuf[k, 0].astype(F32)).astype(BF)
        mail.post(sbuf.at[k, 4], rbuf.at[k, 2], RS + 3 * k + 2, xpeer[d])

    def third(k):
        mail.take(rbuf.at[k, 1], RS + 3 * k + 1)
        mail.take(rbuf.at[k, 2], RS + 3 * k + 2)
        total = sbuf[k, 3].astype(F32) + rbuf[k, 1].astype(F32) + rbuf[k, 2].astype(F32)
        act[k, x] = jax.nn.silu(total).astype(BF)
        for d in (1, -1):
            mail.post(act.at[k, x], act.at[k, x], ACT + 4 * k + x, xpeer[d])

    def fourth(k):
        d = way[k]
        mail.take(act.at[k, xs[-d]], ACT + 4 * k + xs[-d])
        mail.post(act.at[k, xs[-d]], act.at[k, xs[-d]], ACT + 4 * k + xs[-d], xpeer[d])

    def down(k):
        d = way[k]
        mail.take(act.at[k, xs[d]], ACT + 4 * k + xs[d])
        mail.take(act.at[k, xs[2]], ACT + 4 * k + xs[2])
        for f in range(2):
            total = dot(act[k, 0], wd[f, 0:ff])
            for q in range(1, NX):
                total += dot(act[k, q], wd[f, q * ff:(q + 1) * ff])
            prod[k, f] = total.astype(BF)

    steps = [("g", 0), ("a", 0), ("g", 1), ("g", 2), ("a", 1), ("b", 0), ("a", 2), ("b", 1), ("c", 0), ("g", 3),
             ("a", 3), ("b", 2), ("c", 1), ("d", 0), ("b", 3), ("c", 2), ("d", 1), ("w", 0), ("e", 0), ("c", 3),
             ("d", 2), ("e", 1), ("d", 3), ("e", 2), ("e", 3)]
    for what, k in steps:
        if what == "g":
            gathered(k)
        elif what == "a":
            first(k)
        elif what == "b":
            second(k)
        elif what == "c":
            third(k)
        elif what == "d":
            fourth(k)
        elif what == "w":
            mail.take(wd.at[1 - c], WD)
        else:
            down(k)

    mail.post(prod.at[3, 0], yc.at[0], YC, ypeer[1])
    mail.post(prod.at[3, 1], yc.at[1], YC + 1, ypeer[-1])
    mail.post(prod.at[1, 1], ys.at[1], YS + 1, ypeer[1])
    mail.post(prod.at[2, 0], ys.at[0], YS, ypeer[-1])
    mail.take(yc.at[0], YC)
    zs[0] = (prod[1, 0].astype(F32) + yc[0].astype(F32)).astype(BF)
    mail.post(zs.at[0], yc.at[2], RET + 21, ypeer[1])
    mail.take(yc.at[1], YC + 1)
    zs[1] = (prod[2, 1].astype(F32) + yc[1].astype(F32)).astype(BF)
    mail.post(zs.at[1], yc.at[3], RET + 22, ypeer[-1])
    mail.take(ys.at[0], YS)
    mail.take(ys.at[1], YS + 1)
    mail.take(yc.at[2], RET + 21)
    mail.take(yc.at[3], RET + 22)

    def over_y(f):
        return prod[0, f].astype(F32) + ys[f].astype(F32) + yc[2 + f].astype(F32)

    zs[2] = over_y(other).astype(BF)
    mail.post(zs.at[2], zr, ZR, zpeer)
    mine = over_y(half)
    mail.take(zr, ZR)
    final = (mine + zr[...].astype(F32)).astype(BF)
    back[...] = dot(loose, final).astype(BF).reshape(back.shape)

    for i, off in zip(groups, order):
        mail.post(back.at[i], ret.at[own_group], RET + own_group, at(2 * i + c, y, x, half),
                  home if off == 0 else None)
    last = pltpu.make_async_copy(back.at[own_group], ret.at[own_group], local.at[NX + 2])
    pl.when(home)(last.start)

    for j in range(1, 8):
        q = lax.rem(exp + j, 8)
        mail.take(lgr.at[q], LG + q)
    lgr[exp] = lgs[...]
    logits = lgr[0]
    for q in range(1, 8):
        logits += lgr[q]
    logits = logits[:, :tokens]
    picked = [jnp.sum(hits[k] * logits, axis=0, keepdims=True) for k in range(2)]
    gates = [jax.nn.sigmoid(picked[0] - picked[1]), jax.nn.sigmoid(picked[1] - picked[0])]
    blend = jnp.where(match[0], gates[0], 0.0) + jnp.where(match[1], gates[1], 0.0)
    upper = blend.astype(BF)
    lower = (blend - upper.astype(F32)).astype(BF)

    pl.when(home)(last.wait)
    for e, off in zip(groups, order):
        mail.take(ret.at[e], RET + e, home if off == 0 else None)
    rows_in = ret[...].reshape(experts * PAD, -1)
    turn = (((0,), (0,)), ((), ()))
    out[...] = (lax.dot_general(upper, rows_in, turn, preferred_element_type=F32)
                + lax.dot_general(lower, rows_in, turn, preferred_element_type=F32)).astype(BF)
    mail.finish()


def experts_of(hidden, router, expert_ids, w_gate, w_down):
    tokens, feats = hidden.shape
    rows, ff = CAP * 8, w_gate.shape[1] // NX
    vm = pl.BlockSpec(memory_space=pltpu.VMEM)
    hbm = pl.BlockSpec(memory_space=pl.ANY)
    return pl.pallas_call(
        expert_kernel,
        out_shape=jax.ShapeDtypeStruct((tokens, feats), BF),
        in_specs=[vm, vm, vm, hbm, hbm],
        out_specs=vm,
        scratch_shapes=[
            pltpu.VMEM((2, NX, feats, ff), BF),
            pltpu.VMEM((2, NX * ff, feats), BF),
            pltpu.VMEM((8, PAD, feats), BF),
            pltpu.VMEM((8, PAD, feats), BF),
            pltpu.VMEM((BATCHES, 2, rows, feats), BF),
            pltpu.VMEM((BATCHES, 5, rows, ff), BF),
            pltpu.VMEM((BATCHES, 3, rows, ff), BF),
            pltpu.VMEM((BATCHES, NX, rows, ff), BF),
            pltpu.VMEM((BATCHES, 2, rows, feats), BF),
            pltpu.VMEM((2, rows, feats), BF),
            pltpu.VMEM((4, rows, feats), BF),
            pltpu.VMEM((3, rows, feats), BF),
            pltpu.VMEM((rows, feats), BF),
            pltpu.VMEM((8, PAD, feats), BF),
            pltpu.VMEM((8, PAD, feats), BF),
            pltpu.VMEM((8, 128), F32),
            pltpu.VMEM((8, 8, 128), F32),
            pltpu.SemaphoreType.DMA((96,)),
            pltpu.SemaphoreType.DMA((96,)),
            pltpu.SemaphoreType.DMA((8,)),
        ],
        compiler_params=pltpu.CompilerParams(collective_id=0, has_side_effects=True,
                                             vmem_limit_bytes=60 * 1024 * 1024),
        name="experts",
    )(hidden, router.T, expert_ids.T, w_gate, w_down)


def passed_along(value, axis, steps):
    count = lax.axis_size(axis)
    first, last = (max(0, -steps), min(count, count - steps))
    return lax.ppermute(value, axis, [(source, source + steps) for source in range(first, last)])


def carried_in(array, axis, join, neutral):
    place = lax.axis_index(axis)
    gathered = jax.tree.map(
        lambda a, kind: lax.all_gather(a.astype(kind), axis), array, (jnp.bfloat16, jnp.bfloat16)
    )
    state = jax.tree.map(lambda a, e: jnp.zeros_like(a) + jnp.asarray(e, a.dtype), array, neutral)

    def one(lap, state):
        return join(
            state,
            jax.tree.map(
                lambda a, own: lax.dynamic_index_in_dim(a, lap, 0, False).astype(own.dtype),
                gathered,
                array,
            ),
        )

    return lax.fori_loop(0, place, one, state)


def link_pairs(earlier, later):
    return (earlier[0] * later[0], later[0] * earlier[1] + later[1])


def mixer_scan(delta, activated, b_rows, c_rows, rates, start_state):
    token_count, channels = delta.shape
    block_len = 16
    block_count = token_count // block_len

    def regroup(values):
        return values.reshape((block_count, block_len) + values.shape[1:])

    def advance(carry, inputs):
        running, product = carry
        step_delta, step_x, step_b, step_c = inputs
        reads = []
        for position in range(block_len):
            factor = jnp.exp(step_delta[position][None, :] * rates)
            running = (
                factor * running
                + step_b[position][:, None] * (step_delta[position] * step_x[position])[None, :]
            )
            product = factor * product
            reads.append(jnp.sum(step_c[position][:, None] * running, axis=0))
        return ((running, product), (jnp.stack(reads),))

    initial = (start_state, jnp.ones(rates.shape, jnp.float32))
    finals, outputs = lax.scan(
        advance, initial, (regroup(delta), regroup(activated), regroup(b_rows), regroup(c_rows))
    )
    readout = outputs[0].reshape(token_count, channels)
    weighted_all = None
    return (readout, weighted_all, finals[0], finals[1])


def local(
    x_in,
    z_gate,
    dt_low,
    dt_weight,
    dt_bias,
    a_log,
    conv_weight,
    conv_bias,
    d_skip,
    b_and_c,
    hidden,
    router,
    expert_ids,
    w_gate,
    w_down,
):
    tok_rows = x_in.shape[0]
    kernel_taps = conv_weight.shape[0]
    edge_rows = passed_along(x_in[tok_rows - (kernel_taps - 1) :], "seq", 1)
    padded = jnp.concatenate([edge_rows, x_in], axis=0).astype(jnp.float32)
    convolved = jnp.zeros(x_in.shape, jnp.float32) + conv_bias[None, :]
    for offset in range(kernel_taps):
        convolved = convolved + conv_weight[offset][None, :] * padded[offset : offset + tok_rows]
    activated = jax.nn.silu(convolved)
    delta = jax.nn.softplus(
        jnp.dot(dt_low, dt_weight, preferred_element_type=jnp.float32) + dt_bias[None, :]
    )
    rates = -jnp.exp(a_log)
    b_rows = b_and_c[0].T
    c_rows = b_and_c[1].T
    zero_state = jnp.zeros(rates.shape, jnp.float32)
    readout, weighted_all, end_state, end_product = mixer_scan(
        delta, activated, b_rows, c_rows, rates, zero_state
    )
    identity = (jnp.ones(rates.shape, jnp.float32), jnp.zeros(rates.shape, jnp.float32))
    carried = carried_in((end_product, end_state), "seq", link_pairs, identity)
    entering = carried[1]
    readout = mixer_scan(delta, activated, b_rows, c_rows, rates, entering)[0]
    mamba_out = (
        (readout + d_skip[None, :] * activated) * jax.nn.silu(z_gate.astype(jnp.float32))
    ).astype(jnp.bfloat16)
    moe_out = experts_of(hidden, router, expert_ids, w_gate, w_down)
    return (mamba_out, moe_out)


def solution(mesh):
    return jax.shard_map(
        local,
        mesh=mesh,
        in_specs=(
            P("seq", "exp"),
            P("seq", "exp"),
            P("seq", None),
            P(None, "exp"),
            P("exp"),
            P(None, "exp"),
            P(None, "exp"),
            P("exp"),
            P("exp"),
            P(None, None, "seq"),
            P("seq", "exp"),
            P("exp", None),
            P("seq", None),
            P("exp", "seq"),
            P("seq", "exp"),
        ),
        out_specs=(P("seq", "exp"), P("seq", "exp")),
        check_vma=False,
    )
```

```python
import functools

import jax
import jax.numpy as jnp
from jax import lax
from jax.experimental import pallas as pl
from jax.experimental.pallas import tpu as pltpu
from jax.sharding import PartitionSpec as P

CAP = 18
PAD = 32
NZ, NY, NX = 16, 4, 4
MESH = pl.DeviceIdType.MESH
BF, F32 = jnp.bfloat16, jnp.float32
BATCHES = 4


def dot(a, b):
    return jnp.dot(a, b, preferred_element_type=F32)


class Mail:
    def __init__(self, send, recv):
        self.send, self.recv, self.count, self.sent = send, recv, 0, []

    def post(self, src, dst, slot, to, unless=None):
        copy = pltpu.make_async_remote_copy(
            src_ref=src, dst_ref=dst, send_sem=self.send.at[self.count], recv_sem=self.recv.at[slot],
            device_id=to, device_id_type=MESH)
        self.count += 1
        self.sent.append((copy, unless))
        if unless is None:
            copy.start()
        else:
            pl.when(jnp.logical_not(unless))(copy.start)

    def take(self, dst, slot, unless=None):
        copy = pltpu.make_async_remote_copy(
            src_ref=dst, dst_ref=dst, send_sem=self.send.at[0], recv_sem=self.recv.at[slot],
            device_id=(lax.axis_index("seq"), lax.axis_index("exp")), device_id_type=MESH)
        if unless is None:
            copy.wait_recv()
        else:
            pl.when(jnp.logical_not(unless))(copy.wait_recv)

    def finish(self):
        for copy, unless in self.sent:
            if unless is None:
                copy.wait_send()
            else:
                pl.when(jnp.logical_not(unless))(copy.wait_send)


def layer_kernel(x_in, z_gate, dt_low, dt_weight, dt_bias, a_log, conv_weight, conv_bias, d_skip, b_and_c,
                 hid, router_t, ids_t, wg_in, wd_in, mixed, out,
                 wg, wd, pack, in1, rt, sbuf, rbuf, act, prod, ys, yc, zs, zr, back, ret, lgs, lgr,
                 tail, padded, active, delta, drive, rates, factor, state, rowend, rowall, zall, entry, reads,
                 send, recv, local):
    seq, exp = lax.axis_index("seq"), lax.axis_index("exp")
    z, y, x, c = seq // NY, lax.rem(seq, NY), exp // 2, lax.rem(exp, 2)
    half = lax.rem(z, 2)
    zpair = z + 1 - 2 * half
    near = {1: lax.rem(y + 1, NY), -1: lax.rem(y + NY - 1, NY)}
    xs = {d: lax.rem(x + d + NX, NX) for d in (-1, 0, 1, 2)}
    ff = wg.shape[3]

    def at(z_, y_, x_, c_):
        return (z_ * NY + y_, x_ * 2 + c_)

    mate = at(z, y, x, 1 - c)
    ypeer = {d: at(z, near[d], x, c) for d in (1, -1)}
    xpeer = {d: at(z, y, xs[d], c) for d in (1, -1)}
    zpeer = at(zpair, y, x, c)
    experts = 8

    barrier = pltpu.get_barrier_semaphore()
    home = half == c

    def greet(to):
        pl.semaphore_signal(barrier, inc=1, device_id=to, device_id_type=MESH)

    order = [4, 3, 5, 2, 6, 1, 7, 0]
    groups = [lax.rem(z // 2 + off, experts) for off in order]
    for e, off in zip(groups, order):
        to = at(2 * e + c, y, x, half)
        if off == 0:
            pl.when(jnp.logical_not(home))(functools.partial(greet, to))
        else:
            greet(to)
    for to in (zpeer, ypeer[1], ypeer[-1]):
        greet(to)
    for j in range(1, 8):
        greet((seq, lax.rem(exp + j, 8)))
    yfar = lax.rem(y + 2, NY)
    greet(at(z, yfar, x, c))
    starts, ends = seq == 0, seq == NZ * NY - 1
    pl.when(jnp.logical_not(starts))(functools.partial(greet, (seq - jnp.where(starts, 0, 1), exp)))

    def greet_earlier(other_z, carry):
        greet(at(other_z, y, x, c))
        return carry

    lax.fori_loop(0, z, greet_earlier, 0)

    loads = []
    for q in range(NX):
        loads.append(pltpu.make_async_copy(wg_in.at[:, pl.ds(q * ff, ff)], wg.at[c, q], local.at[q]))
    loads.append(pltpu.make_async_copy(wd_in, wd.at[c], local.at[NX]))
    for copy in loads:
        copy.start()

    ids = ids_t[...]
    tokens = ids.shape[1]
    e_iota = lax.broadcasted_iota(jnp.int32, (experts, tokens), 0)
    hits = [(ids[k:k + 1, :] == e_iota).astype(F32) for k in range(2)]
    ahead = (lax.broadcasted_iota(jnp.int32, (tokens, tokens), 0)
             < lax.broadcasted_iota(jnp.int32, (tokens, tokens), 1)).astype(BF)
    before = dot((hits[0] + hits[1]).astype(BF), ahead)
    keys = [ids[k:k + 1, :] * PAD + jnp.sum(hits[k] * before, axis=0, keepdims=True).astype(jnp.int32)
            for k in range(2)]
    r_iota = lax.broadcasted_iota(jnp.int32, (experts * PAD, tokens), 0)
    match = [r_iota == keys[k] for k in range(2)]
    selector = jnp.where(match[0] | match[1], 1.0, 0.0).astype(BF)
    h = hid[...]
    pack[...] = dot(selector, h).astype(BF).reshape(pack.shape)
    lg = lax.dot_general(router_t[...], h, (((1,), (1,)), ((), ())), preferred_element_type=F32)
    lgs[...] = jnp.concatenate([lg, jnp.zeros((experts, 128 - tokens), F32)], axis=1)
    rows = CAP * experts
    r_c = lax.broadcasted_iota(jnp.int32, (rows, experts * PAD), 0)
    q_c = lax.broadcasted_iota(jnp.int32, (rows, experts * PAD), 1)
    group = sum((r_c >= CAP * m).astype(jnp.int32) for m in range(1, experts))
    tight = jnp.where(q_c == r_c + (PAD - CAP) * group, 1.0, 0.0).astype(BF)
    q_e = lax.broadcasted_iota(jnp.int32, (experts * PAD, rows), 0)
    r_e = lax.broadcasted_iota(jnp.int32, (experts * PAD, rows), 1)
    group_e = sum((r_e >= CAP * m).astype(jnp.int32) for m in range(1, experts))
    loose = jnp.where(q_e == r_e + (PAD - CAP) * group_e, 1.0, 0.0).astype(BF)

    channels = x_in.shape[1]
    tiles = channels // 128

    def tiled(ref, values):
        for j in range(tiles):
            ref[:, j, :] = values[:, j * 128:(j + 1) * 128]

    step = jax.nn.softplus(dot(dt_low[...], dt_weight[...]) + dt_bias[...])
    tiled(delta, step)
    tiled(rates, -jnp.exp(a_log[...]))

    mail = Mail(send, recv)
    pl.semaphore_wait(barrier, 8 + 3 + 7 + 1 - home.astype(jnp.int32) + jnp.where(ends, 0, 1) + NZ - 1 - z)

    IN1, RT, RS, ACT = 0, 8, 16, 28
    YS, YC, ZR, RET, LG, WG, WD = 44, 46, 48, 49, 57, 65, 69
    TAIL, ROW, ZALL, ENTRY = 72, 73, 77, 93

    for e, off in zip(groups, order):
        mail.post(pack.at[e], in1.at[z // 2], IN1 + z // 2, at(2 * e + c, y, x, half),
                  home if off == 0 else None)
    mail.post(x_in.at[pl.ds(tokens - 16, 16)], tail, TAIL, (seq + jnp.where(ends, 0, 1), exp), ends)
    own_group = z // 2
    stay = pltpu.make_async_copy(pack.at[own_group], in1.at[own_group], local.at[NX + 1])
    pl.when(home)(stay.start)
    for q in range(NX):
        mail.post(wg_in.at[:, pl.ds(q * ff, ff)], wg.at[c, q], WG + q, mate)
    mail.post(wd_in, wd.at[c], WD, mate)
    for j in range(1, 8):
        mail.post(lgs, lgr.at[exp], LG + exp, (seq, lax.rem(exp + j, 8)))
    mail.take(tail, TAIL, starts)
    before_rows = tail[...].astype(F32)[8:16]
    padded[0:8] = jnp.where(starts, 0.0, before_rows)
    padded[8:8 + tokens] = x_in[...].astype(F32)
    taps = conv_weight.shape[0]
    convolved = conv_bias[...]
    for k in range(taps):
        convolved = convolved + conv_weight[k:k + 1, :] * padded[9 - taps + k:9 - taps + k + tokens]
    activated = jax.nn.silu(convolved)
    active[...] = activated
    tiled(drive, step * activated)
    states = rates.shape[0]

    def own_step(t, carry):
        d, u = delta[t], drive[t]
        values = []
        for n in range(states):
            f = jnp.exp(d * rates[n])
            factor[t, n] = f
            values.append(f * carry[n] + b_and_c[0, n, t] * u)
        return tuple(values) + (carry[states] + d,)

    blank = jnp.zeros((tiles, 128), F32)
    final_state = lax.fori_loop(0, tokens, own_step, (blank,) * (states + 1))
    for n in range(states + 1):
        rowend[y, n] = final_state[n]
    for i, to_y in enumerate((near[1], near[-1], yfar)):
        mail.post(rowend.at[y], rowend.at[y], ROW + y, at(z, to_y, x, c))

    pl.when(home)(stay.wait)
    for e, off in zip(groups, order):
        mail.take(in1.at[e], IN1 + e, home if off == 0 else None)

    rt[0, half] = dot(tight, in1[...].reshape(experts * PAD, -1)).astype(BF)
    other = 1 - half
    mail.post(rt.at[0, half], rt.at[0, half], RT + half, zpeer)
    mail.post(rt.at[0, half], rt.at[2, half], RT + 4 + half, ypeer[1])
    mail.post(rt.at[0, half], rt.at[1, half], RT + 2 + half, ypeer[-1])
    mail.take(rt.at[0, other], RT + other)
    mail.post(rt.at[0, other], rt.at[2, other], RT + 4 + other, ypeer[1])
    mail.post(rt.at[0, other], rt.at[1, other], RT + 2 + other, ypeer[-1])
    quarter = states // NY
    for to_y in (near[1], near[-1], yfar):
        mail.take(rowend.at[to_y], ROW + to_y)
    ahead_sum, row_sum = blank, blank
    for other_y in range(NY):
        ahead_sum = jnp.where(y == other_y, row_sum, ahead_sum)
        row_sum = row_sum + rowend[other_y, states]
    for n in range(states):
        total, mine_before = blank, blank
        for other_y in range(NY):
            mine_before = jnp.where(y == other_y, total, mine_before)
            total = jnp.exp(rates[n] * rowend[other_y, states]) * total + rowend[other_y, n]
        state[n] = mine_before
        rowall[n // quarter, n % quarter] = total
    for i in range(NY):
        rowall[i, quarter] = row_sum
    for later in range(1, NZ):
        gone = z + later >= NZ
        mail.post(rowall.at[y], zall.at[z], ZALL + z, at(jnp.where(gone, z, z + later), y, x, c), gone)

    def along_z():
        def fold(other_z, carry):
            mail.take(zall.at[other_z], ZALL + other_z)
            decay = zall[other_z, quarter]
            return tuple(jnp.exp(rates[quarter * y + i] * decay) * carry[i] + zall[other_z, i]
                         for i in range(quarter))

        entering = lax.fori_loop(0, z, fold, (blank,) * quarter)
        for i in range(quarter):
            entry[y, i] = entering[i]
        for to_y in (near[1], near[-1], yfar):
            mail.post(entry.at[y], entry.at[y], ENTRY + y, at(z, to_y, x, c))

    def enter():
        for to_y in (near[1], near[-1], yfar):
            mail.take(entry.at[to_y], ENTRY + to_y)
        for n in range(states):
            state[n] = state[n] + jnp.exp(rates[n] * ahead_sum) * entry[n // quarter, n % quarter]

    pieces = 4

    def scan_piece(piece):
        def full_step(t, carry):
            u = drive[t]
            values, seen = [], None
            for n in range(states):
                value = factor[t, n] * carry[n] + b_and_c[0, n, t] * u
                values.append(value)
                term = b_and_c[1, n, t] * value
                seen = term if seen is None else seen + term
            reads[t] = seen
            return tuple(values)

        length = tokens // pieces
        done = lax.fori_loop(piece * length, (piece + 1) * length, full_step,
                             tuple(state[n] for n in range(states)))
        for n in range(states):
            state[n] = done[n]

    def finish_mixer():
        for j in range(tiles):
            cols = slice(j * 128, (j + 1) * 128)
            gate = jax.nn.silu(z_gate[:, cols].astype(F32))
            mixed[:, cols] = ((reads[:, j, :] + d_skip[:, cols] * active[:, cols]) * gate).astype(BF)

    for copy in loads:
        copy.wait()
    for q in range(NX):
        mail.take(wg.at[1 - c, q], WG + q)

    def gathered(k):
        if k == 1:
            mail.take(rt.at[1, 1], RT + 3)
            mail.post(rt.at[1, 1], rt.at[3, 1], RT + 7, ypeer[-1])
            mail.take(rt.at[1, 0], RT + 2)
        elif k == 2:
            mail.take(rt.at[2, 0], RT + 4)
            mail.post(rt.at[2, 0], rt.at[3, 0], RT + 6, ypeer[1])
            mail.take(rt.at[2, 1], RT + 5)
        elif k == 3:
            mail.take(rt.at[3, 0], RT + 6)
            mail.take(rt.at[3, 1], RT + 7)

    def part(k, q):
        return dot(rt[k, 0], wg[0, q]) + dot(rt[k, 1], wg[1, q])

    way = [1 if k % 2 == 0 else -1 for k in range(BATCHES)]
    kept = {}

    def first(k):
        d = way[k]
        sbuf[k, 0] = part(k, xs[2]).astype(BF)
        mail.post(sbuf.at[k, 0], rbuf.at[k, 0], RS + 3 * k, xpeer[d])
        sbuf[k, 1] = part(k, xs[-d]).astype(BF)
        mail.post(sbuf.at[k, 1], rbuf.at[k, 1], RS + 3 * k + 1, xpeer[-d])
        sbuf[k, 2] = part(k, xs[d]).astype(BF)
        sbuf[k, 3] = part(k, x).astype(BF)

    def second(k):
        d = way[k]
        mail.take(rbuf.at[k, 0], RS + 3 * k)
        sbuf[k, 4] = (sbuf[k, 2].astype(F32) + rbuf[k, 0].astype(F32)).astype(BF)
        mail.post(sbuf.at[k, 4], rbuf.at[k, 2], RS + 3 * k + 2, xpeer[d])

    def third(k):
        mail.take(rbuf.at[k, 1], RS + 3 * k + 1)
        mail.take(rbuf.at[k, 2], RS + 3 * k + 2)
        total = sbuf[k, 3].astype(F32) + rbuf[k, 1].astype(F32) + rbuf[k, 2].astype(F32)
        act[k, x] = jax.nn.silu(total).astype(BF)
        for d in (1, -1):
            mail.post(act.at[k, x], act.at[k, x], ACT + 4 * k + x, xpeer[d])

    def fourth(k):
        d = way[k]
        mail.take(act.at[k, xs[-d]], ACT + 4 * k + xs[-d])
        mail.post(act.at[k, xs[-d]], act.at[k, xs[-d]], ACT + 4 * k + xs[-d], xpeer[d])

    def down(k):
        d = way[k]
        mail.take(act.at[k, xs[d]], ACT + 4 * k + xs[d])
        mail.take(act.at[k, xs[2]], ACT + 4 * k + xs[2])
        for f in range(2):
            total = dot(act[k, 0], wd[f, 0:ff])
            for q in range(1, NX):
                total += dot(act[k, q], wd[f, q * ff:(q + 1) * ff])
            prod[k, f] = total.astype(BF)

    steps = [("g", 0), ("a", 0), ("g", 1), ("g", 2), ("a", 1), ("b", 0), ("z", 0), ("a", 2), ("b", 1), ("c", 0),
             ("g", 3), ("a", 3), ("b", 2), ("c", 1), ("d", 0), ("y", 0), ("b", 3), ("c", 2), ("m", 0), ("d", 1),
             ("w", 0), ("e", 0), ("m", 1), ("c", 3), ("d", 2), ("e", 1), ("m", 2), ("d", 3), ("e", 2), ("m", 3),
             ("e", 3)]
    for what, k in steps:
        if what == "g":
            gathered(k)
        elif what == "a":
            first(k)
        elif what == "b":
            second(k)
        elif what == "c":
            third(k)
        elif what == "d":
            fourth(k)
        elif what == "z":
            along_z()
        elif what == "y":
            enter()
        elif what == "m":
            scan_piece(k)
        elif what == "w":
            mail.take(wd.at[1 - c], WD)
        else:
            down(k)

    mail.post(prod.at[3, 0], yc.at[0], YC, ypeer[1])
    mail.post(prod.at[3, 1], yc.at[1], YC + 1, ypeer[-1])
    mail.post(prod.at[1, 1], ys.at[1], YS + 1, ypeer[1])
    mail.post(prod.at[2, 0], ys.at[0], YS, ypeer[-1])
    mail.take(yc.at[0], YC)
    zs[0] = (prod[1, 0].astype(F32) + yc[0].astype(F32)).astype(BF)
    mail.post(zs.at[0], yc.at[2], RET + 21, ypeer[1])
    mail.take(yc.at[1], YC + 1)
    zs[1] = (prod[2, 1].astype(F32) + yc[1].astype(F32)).astype(BF)
    mail.post(zs.at[1], yc.at[3], RET + 22, ypeer[-1])
    mail.take(ys.at[0], YS)
    mail.take(ys.at[1], YS + 1)
    mail.take(yc.at[2], RET + 21)
    mail.take(yc.at[3], RET + 22)

    def over_y(f):
        return prod[0, f].astype(F32) + ys[f].astype(F32) + yc[2 + f].astype(F32)

    zs[2] = over_y(other).astype(BF)
    mail.post(zs.at[2], zr, ZR, zpeer)
    mine = over_y(half)
    mail.take(zr, ZR)
    final = (mine + zr[...].astype(F32)).astype(BF)
    back[...] = dot(loose, final).astype(BF).reshape(back.shape)

    for i, off in zip(groups, order):
        mail.post(back.at[i], ret.at[own_group], RET + own_group, at(2 * i + c, y, x, half),
                  home if off == 0 else None)
    last = pltpu.make_async_copy(back.at[own_group], ret.at[own_group], local.at[NX + 2])
    pl.when(home)(last.start)

    finish_mixer()
    for j in range(1, 8):
        q = lax.rem(exp + j, 8)
        mail.take(lgr.at[q], LG + q)
    lgr[exp] = lgs[...]
    logits = lgr[0]
    for q in range(1, 8):
        logits += lgr[q]
    logits = logits[:, :tokens]
    picked = [jnp.sum(hits[k] * logits, axis=0, keepdims=True) for k in range(2)]
    gates = [jax.nn.sigmoid(picked[0] - picked[1]), jax.nn.sigmoid(picked[1] - picked[0])]
    blend = jnp.where(match[0], gates[0], 0.0) + jnp.where(match[1], gates[1], 0.0)
    upper = blend.astype(BF)
    lower = (blend - upper.astype(F32)).astype(BF)

    pl.when(home)(last.wait)
    for e, off in zip(groups, order):
        mail.take(ret.at[e], RET + e, home if off == 0 else None)
    rows_in = ret[...].reshape(experts * PAD, -1)
    turn = (((0,), (0,)), ((), ()))
    out[...] = (lax.dot_general(upper, rows_in, turn, preferred_element_type=F32)
                + lax.dot_general(lower, rows_in, turn, preferred_element_type=F32)).astype(BF)
    mail.finish()


def local(x_in, z_gate, dt_low, dt_weight, dt_bias, a_log, conv_weight, conv_bias, d_skip, b_and_c,
          hidden, router, expert_ids, w_gate, w_down):
    tokens, feats = hidden.shape
    channels, states = x_in.shape[1], a_log.shape[0]
    tiles, quarter = channels // 128, states // NY
    rows, ff = CAP * 8, w_gate.shape[1] // NX
    vm = pl.BlockSpec(memory_space=pltpu.VMEM)
    hbm = pl.BlockSpec(memory_space=pl.ANY)
    sm = pl.BlockSpec(memory_space=pltpu.SMEM)

    def row(a):
        return a.reshape(1, channels)

    return pl.pallas_call(
        layer_kernel,
        out_shape=(jax.ShapeDtypeStruct((tokens, channels), BF), jax.ShapeDtypeStruct((tokens, feats), BF)),
        in_specs=[vm] * 9 + [sm] + [vm] * 3 + [hbm] * 2,
        out_specs=(vm, vm),
        scratch_shapes=[
            pltpu.VMEM((2, NX, feats, ff), BF),
            pltpu.VMEM((2, NX * ff, feats), BF),
            pltpu.VMEM((8, PAD, feats), BF),
            pltpu.VMEM((8, PAD, feats), BF),
            pltpu.VMEM((BATCHES, 2, rows, feats), BF),
            pltpu.VMEM((BATCHES, 5, rows, ff), BF),
            pltpu.VMEM((BATCHES, 3, rows, ff), BF),
            pltpu.VMEM((BATCHES, NX, rows, ff), BF),
            pltpu.VMEM((BATCHES, 2, rows, feats), BF),
            pltpu.VMEM((2, rows, feats), BF),
            pltpu.VMEM((4, rows, feats), BF),
            pltpu.VMEM((3, rows, feats), BF),
            pltpu.VMEM((rows, feats), BF),
            pltpu.VMEM((8, PAD, feats), BF),
            pltpu.VMEM((8, PAD, feats), BF),
            pltpu.VMEM((8, 128), F32),
            pltpu.VMEM((8, 8, 128), F32),
            pltpu.VMEM((16, channels), BF),
            pltpu.VMEM((8 + tokens, channels), F32),
            pltpu.VMEM((tokens, channels), F32),
            pltpu.VMEM((tokens, tiles, 128), F32),
            pltpu.VMEM((tokens, tiles, 128), F32),
            pltpu.VMEM((states, tiles, 128), F32),
            pltpu.VMEM((tokens, states, tiles, 128), F32),
            pltpu.VMEM((states, tiles, 128), F32),
            pltpu.VMEM((NY, states + 1, tiles, 128), F32),
            pltpu.VMEM((NY, quarter + 1, tiles, 128), F32),
            pltpu.VMEM((NZ, quarter + 1, tiles, 128), F32),
            pltpu.VMEM((NY, quarter, tiles, 128), F32),
            pltpu.VMEM((tokens, tiles, 128), F32),
            pltpu.SemaphoreType.DMA((128,)),
            pltpu.SemaphoreType.DMA((128,)),
            pltpu.SemaphoreType.DMA((8,)),
        ],
        compiler_params=pltpu.CompilerParams(collective_id=0, has_side_effects=True,
                                             vmem_limit_bytes=60 * 1024 * 1024),
        name="layer",
    )(x_in, z_gate, dt_low, dt_weight, row(dt_bias), a_log, conv_weight, row(conv_bias), row(d_skip), b_and_c,
      hidden, router.T, expert_ids.T, w_gate, w_down)


def solution(mesh):
    return jax.shard_map(
        local,
        mesh=mesh,
        in_specs=(
            P("seq", "exp"),
            P("seq", "exp"),
            P("seq", None),
            P(None, "exp"),
            P("exp"),
            P(None, "exp"),
            P(None, "exp"),
            P("exp"),
            P("exp"),
            P(None, None, "seq"),
            P("seq", "exp"),
            P("exp", None),
            P("seq", None),
            P("exp", "seq"),
            P("seq", "exp"),
        ),
        out_specs=(P("seq", "exp"), P("seq", "exp")),
        check_vma=False,
    )
```

```python
import functools

import jax
import jax.numpy as jnp
from jax import lax
from jax.experimental import pallas as pl
from jax.experimental.pallas import tpu as pltpu
from jax.sharding import PartitionSpec as P

CAP = 18
PAD = 24
NZ, NY, NX = 16, 4, 4
MESH = pl.DeviceIdType.MESH
BF, F32 = jnp.bfloat16, jnp.float32
BATCHES = ((0, 0, 80), (1, 0, 144), (3, 0, 144), (2, 0, 144), (0, 80, 64))


def dot(a, b):
    return jnp.dot(a, b, preferred_element_type=F32)


class Mail:
    def __init__(self, send, recv):
        self.send, self.recv, self.count, self.sent = send, recv, 0, []

    def post(self, src, dst, slot, to, unless=None):
        copy = pltpu.make_async_remote_copy(
            src_ref=src, dst_ref=dst, send_sem=self.send.at[self.count], recv_sem=self.recv.at[slot],
            device_id=to, device_id_type=MESH)
        self.count += 1
        self.sent.append((copy, unless))
        if unless is None:
            copy.start()
        else:
            pl.when(jnp.logical_not(unless))(copy.start)

    def take(self, dst, slot, unless=None):
        copy = pltpu.make_async_remote_copy(
            src_ref=dst, dst_ref=dst, send_sem=self.send.at[0], recv_sem=self.recv.at[slot],
            device_id=(lax.axis_index("seq"), lax.axis_index("exp")), device_id_type=MESH)
        if unless is None:
            copy.wait_recv()
        else:
            pl.when(jnp.logical_not(unless))(copy.wait_recv)

    def finish(self):
        for copy, unless in self.sent:
            if unless is None:
                copy.wait_send()
            else:
                pl.when(jnp.logical_not(unless))(copy.wait_send)


def layer_kernel(x_in, z_gate, dt_low, dt_weight, dt_bias, a_log, conv_weight, conv_bias, d_skip, b_and_c,
                 hid, router_t, ids_t, wg_in, wd_in, mixed, out,
                 wg, wd, pack, in1, rt, sbuf, rbuf, act, prod, ys, yc, zs, zr, back, ret, lgs, lgr,
                 tail, padded, active, delta, drive, rates, factor, state, rowend, rowall, zall, entry, reads,
                 send, recv, local):
    seq, exp = lax.axis_index("seq"), lax.axis_index("exp")
    z, y, x, c = seq // NY, lax.rem(seq, NY), exp // 2, lax.rem(exp, 2)
    half = lax.rem(z, 2)
    zpair = z + 1 - 2 * half
    near = {1: lax.rem(y + 1, NY), -1: lax.rem(y + NY - 1, NY)}
    xs = {d: lax.rem(x + d + NX, NX) for d in (-1, 0, 1, 2)}
    ff = wg.shape[3]

    def at(z_, y_, x_, c_):
        return (z_ * NY + y_, x_ * 2 + c_)

    mate = at(z, y, x, 1 - c)
    ypeer = {d: at(z, near[d], x, c) for d in (1, -1)}
    xpeer = {d: at(z, y, xs[d], c) for d in (1, -1)}
    zpeer = at(zpair, y, x, c)
    experts = 8

    barrier = pltpu.get_barrier_semaphore()
    home = half == c

    def greet(to):
        pl.semaphore_signal(barrier, inc=1, device_id=to, device_id_type=MESH)

    order = [4, 3, 5, 2, 6, 1, 7, 0]
    groups = [lax.rem(z // 2 + off, experts) for off in order]
    away = jnp.logical_not(home)

    def unless(cond, work):
        pl.when(jnp.logical_not(cond))(work)

    homes = [at(2 * e + half, y, x, half) for e in groups]
    for to, off in zip(homes, order):
        if off == 0:
            unless(home, functools.partial(greet, to))
        else:
            greet(to)
    feeds = [(f, e, off, at(2 * e + c, y, x, f)) for off, e in zip(order, groups) for f in range(2)]

    def greet_feeds():
        for f, e, off, to in feeds:
            if off == 0:
                unless(c == f, functools.partial(greet, to))
            else:
                greet(to)

    pl.when(home)(greet_feeds)
    for to in (zpeer, ypeer[1], ypeer[-1]):
        greet(to)
    for j in range(1, 8):
        greet((seq, lax.rem(exp + j, 8)))
    yfar = lax.rem(y + 2, NY)
    greet(at(z, yfar, x, c))
    starts, ends = seq == 0, seq == NZ * NY - 1
    pl.when(jnp.logical_not(starts))(functools.partial(greet, (seq - jnp.where(starts, 0, 1), exp)))

    def greet_earlier(other_z, carry):
        greet(at(other_z, y, x, c))
        return carry

    lax.fori_loop(0, z, greet_earlier, 0)

    loads = []
    for q in range(NX):
        loads.append(pltpu.make_async_copy(wg_in.at[:, pl.ds(q * ff, ff)], wg.at[c, q], local.at[q]))
    loads.append(pltpu.make_async_copy(wd_in, wd.at[c], local.at[NX]))
    for copy in loads:
        copy.start()

    ids = ids_t[...]
    tokens = ids.shape[1]
    e_iota = lax.broadcasted_iota(jnp.int32, (experts, tokens), 0)
    hits = [(ids[k:k + 1, :] == e_iota).astype(F32) for k in range(2)]
    ahead = (lax.broadcasted_iota(jnp.int32, (tokens, tokens), 0)
             < lax.broadcasted_iota(jnp.int32, (tokens, tokens), 1)).astype(BF)
    before = dot((hits[0] + hits[1]).astype(BF), ahead)
    keys = [ids[k:k + 1, :] * PAD + jnp.sum(hits[k] * before, axis=0, keepdims=True).astype(jnp.int32)
            for k in range(2)]
    r_iota = lax.broadcasted_iota(jnp.int32, (experts * PAD, tokens), 0)
    match = [r_iota == keys[k] for k in range(2)]
    selector = jnp.where(match[0] | match[1], 1.0, 0.0).astype(BF)
    h = hid[...]
    pack[...] = dot(selector, h).astype(BF).reshape(pack.shape)
    lg = lax.dot_general(router_t[...], h, (((1,), (1,)), ((), ())), preferred_element_type=F32)
    lgs[...] = jnp.concatenate([lg, jnp.zeros((experts, 128 - tokens), F32)], axis=1)
    rows = CAP * experts
    r_c = lax.broadcasted_iota(jnp.int32, (rows, experts * PAD), 0)
    q_c = lax.broadcasted_iota(jnp.int32, (rows, experts * PAD), 1)
    group = sum((r_c >= CAP * m).astype(jnp.int32) for m in range(1, experts))
    tight = jnp.where(q_c == r_c + (PAD - CAP) * group, 1.0, 0.0).astype(BF)
    q_e = lax.broadcasted_iota(jnp.int32, (experts * PAD, rows), 0)
    r_e = lax.broadcasted_iota(jnp.int32, (experts * PAD, rows), 1)
    group_e = sum((r_e >= CAP * m).astype(jnp.int32) for m in range(1, experts))
    loose = jnp.where(q_e == r_e + (PAD - CAP) * group_e, 1.0, 0.0).astype(BF)

    channels = x_in.shape[1]
    tiles = channels // 128

    def tiled(ref, values):
        for j in range(tiles):
            ref[:, j, :] = values[:, j * 128:(j + 1) * 128]

    step = jax.nn.softplus(dot(dt_low[...], dt_weight[...]) + dt_bias[...])
    tiled(delta, step)
    tiled(rates, -jnp.exp(a_log[...]))

    mail = Mail(send, recv)
    pl.semaphore_wait(barrier, 8 + 3 + 7 + 1 + 14 * home.astype(jnp.int32) + jnp.where(ends, 0, 1) + NZ - 1 - z)

    IN1, RT, RS, ACT = 0, 16, 24, 39
    YS, YC, ZR, RET, LG, WG, WD = 59, 61, 65, 67, 75, 83, 87
    TAIL, ROW, ZALL, ENTRY = 88, 89, 93, 109

    for e, off, to in zip(groups, order, homes):
        mail.post(pack.at[e], in1.at[c, z // 2], IN1 + 8 * c + z // 2, to, home if off == 0 else None)
    mail.post(x_in.at[pl.ds(tokens - 16, 16)], tail, TAIL, (seq + jnp.where(ends, 0, 1), exp), ends)
    own_group = z // 2
    stay = pltpu.make_async_copy(pack.at[own_group], in1.at[c, own_group], local.at[NX + 1])
    pl.when(home)(stay.start)
    for q in range(NX):
        mail.post(wg_in.at[:, pl.ds(q * ff, ff)], wg.at[c, q], WG + q, mate)
    mail.post(wd_in, wd.at[c], WD, mate)
    for j in range(1, 8):
        mail.post(lgs, lgr.at[exp], LG + exp, (seq, lax.rem(exp + j, 8)))
    mail.take(tail, TAIL, starts)
    before_rows = tail[...].astype(F32)[8:16]
    padded[0:8] = jnp.where(starts, 0.0, before_rows)
    padded[8:8 + tokens] = x_in[...].astype(F32)
    taps = conv_weight.shape[0]
    convolved = conv_bias[...]
    for k in range(taps):
        convolved = convolved + conv_weight[k:k + 1, :] * padded[9 - taps + k:9 - taps + k + tokens]
    activated = jax.nn.silu(convolved)
    active[...] = activated
    tiled(drive, step * activated)
    states = rates.shape[0]

    def own_step(t, carry):
        d, u = delta[t], drive[t]
        values = []
        for n in range(states):
            f = jnp.exp(d * rates[n])
            factor[t, n] = f
            values.append(f * carry[n] + b_and_c[0, n, t] * u)
        return tuple(values) + (carry[states] + d,)

    blank = jnp.zeros((tiles, 128), F32)
    final_state = lax.fori_loop(0, tokens, own_step, (blank,) * (states + 1))
    for n in range(states + 1):
        rowend[y, n] = final_state[n]
    for i, to_y in enumerate((near[1], near[-1], yfar)):
        mail.post(rowend.at[y], rowend.at[y], ROW + y, at(z, to_y, x, c))

    pl.when(home)(stay.wait)
    for f, e, off, to in feeds:
        mail.take(in1.at[f, e], IN1 + 8 * f + e, (away | (c == f)) if off == 0 else away)

    def compact():
        for f in range(2):
            rt[0, f] = dot(tight, in1[f].reshape(experts * PAD, -1)).astype(BF)

    pl.when(home)(compact)
    for f in range(2):
        mail.post(rt.at[0, f], rt.at[0, f], RT + f, zpeer, away)
    for f in range(2):
        mail.take(rt.at[0, f], RT + f, home)
        mail.post(rt.at[0, f], rt.at[2, f], RT + 4 + f, ypeer[1])
        mail.post(rt.at[0, f], rt.at[1, f], RT + 2 + f, ypeer[-1])
    quarter = states // NY
    for to_y in (near[1], near[-1], yfar):
        mail.take(rowend.at[to_y], ROW + to_y)
    ahead_sum, row_sum = blank, blank
    for other_y in range(NY):
        ahead_sum = jnp.where(y == other_y, row_sum, ahead_sum)
        row_sum = row_sum + rowend[other_y, states]
    for n in range(states):
        total, mine_before = blank, blank
        for other_y in range(NY):
            mine_before = jnp.where(y == other_y, total, mine_before)
            total = jnp.exp(rates[n] * rowend[other_y, states]) * total + rowend[other_y, n]
        state[n] = mine_before
        rowall[n // quarter, n % quarter] = total
    for i in range(NY):
        rowall[i, quarter] = row_sum
    for later in range(1, NZ):
        gone = z + later >= NZ
        mail.post(rowall.at[y], zall.at[z], ZALL + z, at(jnp.where(gone, z, z + later), y, x, c), gone)

    def along_z():
        def fold(other_z, carry):
            mail.take(zall.at[other_z], ZALL + other_z)
            decay = zall[other_z, quarter]
            return tuple(jnp.exp(rates[quarter * y + i] * decay) * carry[i] + zall[other_z, i]
                         for i in range(quarter))

        entering = lax.fori_loop(0, z, fold, (blank,) * quarter)
        for i in range(quarter):
            entry[y, i] = entering[i]
        for to_y in (near[1], near[-1], yfar):
            mail.post(entry.at[y], entry.at[y], ENTRY + y, at(z, to_y, x, c))

    def enter():
        for to_y in (near[1], near[-1], yfar):
            mail.take(entry.at[to_y], ENTRY + to_y)
        for n in range(states):
            state[n] = state[n] + jnp.exp(rates[n] * ahead_sum) * entry[n // quarter, n % quarter]

    pieces = 4

    def scan_piece(piece):
        def full_step(t, carry):
            u = drive[t]
            values, seen = [], None
            for n in range(states):
                value = factor[t, n] * carry[n] + b_and_c[0, n, t] * u
                values.append(value)
                term = b_and_c[1, n, t] * value
                seen = term if seen is None else seen + term
            reads[t] = seen
            return tuple(values)

        length = tokens // pieces
        done = lax.fori_loop(piece * length, (piece + 1) * length, full_step,
                             tuple(state[n] for n in range(states)))
        for n in range(states):
            state[n] = done[n]

    def finish_mixer():
        for j in range(tiles):
            cols = slice(j * 128, (j + 1) * 128)
            gate = jax.nn.silu(z_gate[:, cols].astype(F32))
            mixed[:, cols] = ((reads[:, j, :] + d_skip[:, cols] * active[:, cols]) * gate).astype(BF)

    for copy in loads:
        copy.wait()
    for q in range(NX):
        mail.take(wg.at[1 - c, q], WG + q)

    def gathered(k):
        if k == 1:
            mail.take(rt.at[1, 1], RT + 3)
            mail.post(rt.at[1, 1], rt.at[3, 1], RT + 7, ypeer[-1])
            mail.take(rt.at[1, 0], RT + 2)
        elif k == 2:
            mail.take(rt.at[2, 0], RT + 4)
            mail.post(rt.at[2, 0], rt.at[3, 0], RT + 6, ypeer[1])
            mail.take(rt.at[2, 1], RT + 5)
        else:
            mail.take(rt.at[3, 0], RT + 6)
            mail.take(rt.at[3, 1], RT + 7)

    def span(b):
        return pl.ds(0, BATCHES[b][2])

    def part(b, q):
        k, start, count = BATCHES[b]
        held = pl.ds(start, count)
        return dot(rt[k, 0, held], wg[0, q]) + dot(rt[k, 1, held], wg[1, q])

    way = [1, -1, 1, -1, 1]

    def first(b):
        d, r = way[b], span(b)
        sbuf[b, 0, r] = part(b, xs[2]).astype(BF)
        mail.post(sbuf.at[b, 0, r], rbuf.at[b, 0, r], RS + 3 * b, xpeer[d])
        sbuf[b, 1, r] = part(b, xs[-d]).astype(BF)
        mail.post(sbuf.at[b, 1, r], rbuf.at[b, 1, r], RS + 3 * b + 1, xpeer[-d])
        sbuf[b, 2, r] = part(b, xs[d]).astype(BF)
        sbuf[b, 3, r] = part(b, x).astype(BF)

    def second(b):
        d, r = way[b], span(b)
        mail.take(rbuf.at[b, 0, r], RS + 3 * b)
        sbuf[b, 4, r] = (sbuf[b, 2, r].astype(F32) + rbuf[b, 0, r].astype(F32)).astype(BF)
        mail.post(sbuf.at[b, 4, r], rbuf.at[b, 2, r], RS + 3 * b + 2, xpeer[d])

    def third(b):
        r = span(b)
        mail.take(rbuf.at[b, 1, r], RS + 3 * b + 1)
        mail.take(rbuf.at[b, 2, r], RS + 3 * b + 2)
        total = sbuf[b, 3, r].astype(F32) + rbuf[b, 1, r].astype(F32) + rbuf[b, 2, r].astype(F32)
        act[b, x, r] = jax.nn.silu(total).astype(BF)
        for d in (1, -1):
            mail.post(act.at[b, x, r], act.at[b, x, r], ACT + 4 * b + x, xpeer[d])

    def fourth(b):
        d, r = way[b], span(b)
        mail.take(act.at[b, xs[-d], r], ACT + 4 * b + xs[-d])
        mail.post(act.at[b, xs[-d], r], act.at[b, xs[-d], r], ACT + 4 * b + xs[-d], xpeer[d])

    def down(b):
        d, r = way[b], span(b)
        k, start, count = BATCHES[b]
        mail.take(act.at[b, xs[d], r], ACT + 4 * b + xs[d])
        mail.take(act.at[b, xs[2], r], ACT + 4 * b + xs[2])
        for f in range(2):
            total = dot(act[b, 0, r], wd[f, 0:ff])
            for q in range(1, NX):
                total += dot(act[b, q, r], wd[f, q * ff:(q + 1) * ff])
            prod[k, f, pl.ds(start, count)] = total.astype(BF)

    def home_far():
        mail.post(prod.at[3, 0], yc.at[0], YC, ypeer[1])
        mail.post(prod.at[3, 1], yc.at[1], YC + 1, ypeer[-1])

    def home_next():
        mail.take(yc.at[0], YC)
        zs[0] = (prod[1, 0].astype(F32) + yc[0].astype(F32)).astype(BF)
        mail.post(zs.at[0], yc.at[2], YC + 2, ypeer[1])

    def home_previous():
        mail.post(prod.at[2, 0], ys.at[0], YS, ypeer[-1])
        mail.take(yc.at[1], YC + 1)
        zs[1] = (prod[2, 1].astype(F32) + yc[1].astype(F32)).astype(BF)
        mail.post(zs.at[1], yc.at[3], YC + 3, ypeer[-1])

    steps = [
        ("first", 0), ("block", 1), ("first", 1), ("second", 0), ("block", 2), ("block", 3), ("first", 2), ("second", 1),
        ("third", 0), ("first", 3), ("second", 2), ("third", 1), ("fourth", 0), ("first", 4), ("second", 3), ("third", 2),
        ("fourth", 1), ("weights", 0), ("down", 0), ("second", 4), ("third", 3), ("fourth", 2), ("down", 1), ("single", 0),
        ("third", 4), ("fourth", 3), ("down", 2), ("far", 0), ("scan", 0), ("fourth", 4), ("next", 0), ("down", 3),
        ("previous", 0), ("down", 4)]
    does = {"first": first, "second": second, "third": third, "fourth": fourth, "down": down, "block": gathered,
            "far": lambda b: home_far(), "next": lambda b: home_next(), "previous": lambda b: home_previous(),
            "single": lambda b: mail.post(prod.at[1, 1], ys.at[1], YS + 1, ypeer[1]),
            "scan": lambda b: along_z(), "weights": lambda b: mail.take(wd.at[1 - c], WD)}
    for what, b in steps:
        does[what](b)
    mail.take(ys.at[0], YS)
    mail.take(ys.at[1], YS + 1)
    mail.take(yc.at[2], YC + 2)
    mail.take(yc.at[3], YC + 3)

    def over_y(f):
        return prod[0, f].astype(F32) + ys[f].astype(F32) + yc[2 + f].astype(F32)

    for f in range(2):
        total = over_y(f)
        zs[2 + f] = total.astype(BF)
        mail.post(zs.at[2 + f], zr.at[f], ZR + f, zpeer, home)
    for f in range(2):
        mail.take(zr.at[f], ZR + f, away)

    def spread():
        for f in range(2):
            whole = (over_y(f) + zr[f].astype(F32)).astype(BF)
            back[f] = dot(loose, whole).astype(BF).reshape(back.shape[1:])

    pl.when(home)(spread)
    for f, e, off, to in feeds:
        mail.post(back.at[f, e], ret.at[own_group], RET + own_group, to, (away | (c == f)) if off == 0 else away)
    last = pltpu.make_async_copy(back.at[c, own_group], ret.at[own_group], local.at[NX + 2])
    pl.when(home)(last.start)

    enter()
    for piece in range(pieces):
        scan_piece(piece)
    finish_mixer()
    for j in range(1, 8):
        q = lax.rem(exp + j, 8)
        mail.take(lgr.at[q], LG + q)
    lgr[exp] = lgs[...]
    logits = lgr[0]
    for q in range(1, 8):
        logits += lgr[q]
    logits = logits[:, :tokens]
    picked = [jnp.sum(hits[k] * logits, axis=0, keepdims=True) for k in range(2)]
    gates = [jax.nn.sigmoid(picked[0] - picked[1]), jax.nn.sigmoid(picked[1] - picked[0])]
    blend = jnp.where(match[0], gates[0], 0.0) + jnp.where(match[1], gates[1], 0.0)
    upper = blend.astype(BF)
    lower = (blend - upper.astype(F32)).astype(BF)

    pl.when(home)(last.wait)
    for e, off in zip(groups, order):
        mail.take(ret.at[e], RET + e, home if off == 0 else None)
    rows_in = ret[...].reshape(experts * PAD, -1)
    turn = (((0,), (0,)), ((), ()))
    out[...] = (lax.dot_general(upper, rows_in, turn, preferred_element_type=F32)
                + lax.dot_general(lower, rows_in, turn, preferred_element_type=F32)).astype(BF)
    mail.finish()


def local(x_in, z_gate, dt_low, dt_weight, dt_bias, a_log, conv_weight, conv_bias, d_skip, b_and_c,
          hidden, router, expert_ids, w_gate, w_down):
    tokens, feats = hidden.shape
    channels, states = x_in.shape[1], a_log.shape[0]
    tiles, quarter = channels // 128, states // NY
    rows, ff = CAP * 8, w_gate.shape[1] // NX
    vm = pl.BlockSpec(memory_space=pltpu.VMEM)
    hbm = pl.BlockSpec(memory_space=pl.ANY)
    sm = pl.BlockSpec(memory_space=pltpu.SMEM)

    def row(a):
        return a.reshape(1, channels)

    return pl.pallas_call(
        layer_kernel,
        out_shape=(jax.ShapeDtypeStruct((tokens, channels), BF), jax.ShapeDtypeStruct((tokens, feats), BF)),
        in_specs=[vm] * 9 + [sm] + [vm] * 3 + [hbm] * 2,
        out_specs=(vm, vm),
        scratch_shapes=[
            pltpu.VMEM((2, NX, feats, ff), BF),
            pltpu.VMEM((2, NX * ff, feats), BF),
            pltpu.VMEM((8, PAD, feats), BF),
            pltpu.VMEM((2, 8, PAD, feats), BF),
            pltpu.VMEM((4, 2, rows, feats), BF),
            pltpu.VMEM((len(BATCHES), 5, rows, ff), BF),
            pltpu.VMEM((len(BATCHES), 3, rows, ff), BF),
            pltpu.VMEM((len(BATCHES), NX, rows, ff), BF),
            pltpu.VMEM((4, 2, rows, feats), BF),
            pltpu.VMEM((2, rows, feats), BF),
            pltpu.VMEM((4, rows, feats), BF),
            pltpu.VMEM((4, rows, feats), BF),
            pltpu.VMEM((2, rows, feats), BF),
            pltpu.VMEM((2, 8, PAD, feats), BF),
            pltpu.VMEM((8, PAD, feats), BF),
            pltpu.VMEM((8, 128), F32),
            pltpu.VMEM((8, 8, 128), F32),
            pltpu.VMEM((16, channels), BF),
            pltpu.VMEM((8 + tokens, channels), F32),
            pltpu.VMEM((tokens, channels), F32),
            pltpu.VMEM((tokens, tiles, 128), F32),
            pltpu.VMEM((tokens, tiles, 128), F32),
            pltpu.VMEM((states, tiles, 128), F32),
            pltpu.VMEM((tokens, states, tiles, 128), F32),
            pltpu.VMEM((states, tiles, 128), F32),
            pltpu.VMEM((NY, states + 1, tiles, 128), F32),
            pltpu.VMEM((NY, quarter + 1, tiles, 128), F32),
            pltpu.VMEM((NZ, quarter + 1, tiles, 128), F32),
            pltpu.VMEM((NY, quarter, tiles, 128), F32),
            pltpu.VMEM((tokens, tiles, 128), F32),
            pltpu.SemaphoreType.DMA((128,)),
            pltpu.SemaphoreType.DMA((128,)),
            pltpu.SemaphoreType.DMA((8,)),
        ],
        compiler_params=pltpu.CompilerParams(collective_id=0, has_side_effects=True,
                                             vmem_limit_bytes=60 * 1024 * 1024),
        name="layer",
    )(x_in, z_gate, dt_low, dt_weight, row(dt_bias), a_log, conv_weight, row(conv_bias), row(d_skip), b_and_c,
      hidden, router.T, expert_ids.T, w_gate, w_down)


def solution(mesh):
    return jax.shard_map(
        local,
        mesh=mesh,
        in_specs=(
            P("seq", "exp"),
            P("seq", "exp"),
            P("seq", None),
            P(None, "exp"),
            P("exp"),
            P(None, "exp"),
            P(None, "exp"),
            P("exp"),
            P("exp"),
            P(None, None, "seq"),
            P("seq", "exp"),
            P("exp", None),
            P("seq", None),
            P("exp", "seq"),
            P("seq", "exp"),
        ),
        out_specs=(P("seq", "exp"), P("seq", "exp")),
        check_vma=False,
    )
```

```python
import functools

import jax
import jax.numpy as jnp
from jax import lax
from jax.experimental import pallas as pl
from jax.experimental.pallas import tpu as pltpu
from jax.sharding import PartitionSpec as P

CAP = 18
PAD = 24
NZ, NY, NX = 16, 4, 4
MESH = pl.DeviceIdType.MESH
BF, F32 = jnp.bfloat16, jnp.float32
SHARE = 4
BATCHES = (((0, 0),), ((1, 0), (2, 0)), ((3, 0), (3, 1)), ((1, 1), (2, 1)), ((0, 1),))


def dot(a, b):
    return jnp.dot(a, b, preferred_element_type=F32)


class Mail:
    def __init__(self, send, recv):
        self.send, self.recv, self.count, self.sent = send, recv, 0, []

    def post(self, src, dst, slot, to, unless=None):
        copy = pltpu.make_async_remote_copy(
            src_ref=src, dst_ref=dst, send_sem=self.send.at[self.count], recv_sem=self.recv.at[slot],
            device_id=to, device_id_type=MESH)
        self.count += 1
        self.sent.append((copy, unless))
        if unless is None:
            copy.start()
        else:
            pl.when(jnp.logical_not(unless))(copy.start)

    def take(self, dst, slot, unless=None):
        copy = pltpu.make_async_remote_copy(
            src_ref=dst, dst_ref=dst, send_sem=self.send.at[0], recv_sem=self.recv.at[slot],
            device_id=(lax.axis_index("seq"), lax.axis_index("exp")), device_id_type=MESH)
        if unless is None:
            copy.wait_recv()
        else:
            pl.when(jnp.logical_not(unless))(copy.wait_recv)

    def finish(self):
        for copy, unless in self.sent:
            if unless is None:
                copy.wait_send()
            else:
                pl.when(jnp.logical_not(unless))(copy.wait_send)


def layer_kernel(x_in, z_gate, dt_low, dt_weight, dt_bias, a_log, conv_weight, conv_bias, d_skip, b_and_c,
                 hid, router_t, ids_t, wg_in, wd_in, mixed, out,
                 wg, wd, pack, in1, rt, sbuf, rbuf, act, prod, ys, yc, zs, zr, back, ret, lgs, lgr, zb,
                 tail, padded, active, delta, drive, rates, factor, state, rowend, rowall, zall, entry, reads,
                 send, recv, local):
    seq, exp = lax.axis_index("seq"), lax.axis_index("exp")
    z, y, x, c = seq // NY, lax.rem(seq, NY), exp // 2, lax.rem(exp, 2)
    half = lax.rem(z, 2)
    zpair = z + 1 - 2 * half
    near = {1: lax.rem(y + 1, NY), -1: lax.rem(y + NY - 1, NY)}
    xs = {d: lax.rem(x + d + NX, NX) for d in (-1, 0, 1, 2)}
    ff = wg.shape[3]

    def at(z_, y_, x_, c_):
        return (z_ * NY + y_, x_ * 2 + c_)

    mate = at(z, y, x, 1 - c)
    ypeer = {d: at(z, near[d], x, c) for d in (1, -1)}
    xpeer = {d: at(z, y, xs[d], c) for d in (1, -1)}
    zpeer = at(zpair, y, x, c)
    experts = 8

    barrier = pltpu.get_barrier_semaphore()

    def greet(to):
        pl.semaphore_signal(barrier, inc=1, device_id=to, device_id_type=MESH)

    def unless(cond, work):
        pl.when(jnp.logical_not(cond))(work)

    order = [4, 3, 5, 2, 6, 1, 7, 0]
    groups = [lax.rem(z // 2 + off, experts) for off in order]
    wide, turn_j = lax.rem(z // 2, 2), z // 4
    mine = (half == c) & (wide == half)
    targets = [(off == 0, e, at(2 * e + wide, y, x, half)) for off, e in zip(order, groups)]
    feeds = [(f, j, at(4 * j + 2 * half + c, y, x, f)) for j in range(SHARE) for f in range(2)]

    def is_me(f, j):
        return mine & (c == f) & (turn_j == j)

    for near_one, e, to in targets:
        if near_one:
            unless(mine, functools.partial(greet, to))
        else:
            greet(to)
    for f, j, to in feeds:
        unless(is_me(f, j), functools.partial(greet, to))
    for to in (zpeer, ypeer[1], ypeer[-1]):
        greet(to)
    for j in range(1, 8):
        greet((seq, lax.rem(exp + j, 8)))
    yfar = lax.rem(y + 2, NY)
    greet(at(z, yfar, x, c))
    starts, ends = seq == 0, seq == NZ * NY - 1
    pl.when(jnp.logical_not(starts))(functools.partial(greet, (seq - jnp.where(starts, 0, 1), exp)))

    def greet_earlier(other_z, carry):
        greet(at(other_z, y, x, c))
        return carry

    lax.fori_loop(0, z, greet_earlier, 0)

    loads = []
    for q in range(NX):
        loads.append(pltpu.make_async_copy(wg_in.at[:, pl.ds(q * ff, ff)], wg.at[c, q], local.at[q]))
    loads.append(pltpu.make_async_copy(wd_in, wd.at[c], local.at[NX]))
    for copy in loads:
        copy.start()

    ids = ids_t[...]
    tokens = ids.shape[1]
    e_iota = lax.broadcasted_iota(jnp.int32, (experts, tokens), 0)
    hits = [(ids[k:k + 1, :] == e_iota).astype(F32) for k in range(2)]
    ahead = (lax.broadcasted_iota(jnp.int32, (tokens, tokens), 0)
             < lax.broadcasted_iota(jnp.int32, (tokens, tokens), 1)).astype(BF)
    before = dot((hits[0] + hits[1]).astype(BF), ahead)
    keys = [ids[k:k + 1, :] * PAD + jnp.sum(hits[k] * before, axis=0, keepdims=True).astype(jnp.int32)
            for k in range(2)]
    r_iota = lax.broadcasted_iota(jnp.int32, (experts * PAD, tokens), 0)
    match = [r_iota == keys[k] for k in range(2)]
    selector = jnp.where(match[0] | match[1], 1.0, 0.0).astype(BF)
    h = hid[...]
    pack[...] = dot(selector, h).astype(BF).reshape(pack.shape)
    lg = lax.dot_general(router_t[...], h, (((1,), (1,)), ((), ())), preferred_element_type=F32)
    lgs[...] = jnp.concatenate([lg, jnp.zeros((experts, 128 - tokens), F32)], axis=1)
    rows = CAP * SHARE
    r_c = lax.broadcasted_iota(jnp.int32, (rows, SHARE * PAD), 0)
    q_c = lax.broadcasted_iota(jnp.int32, (rows, SHARE * PAD), 1)
    group = sum((r_c >= CAP * m).astype(jnp.int32) for m in range(1, SHARE))
    tight = jnp.where(q_c == r_c + (PAD - CAP) * group, 1.0, 0.0).astype(BF)
    q_e = lax.broadcasted_iota(jnp.int32, (SHARE * PAD, rows), 0)
    r_e = lax.broadcasted_iota(jnp.int32, (SHARE * PAD, rows), 1)
    group_e = sum((r_e >= CAP * m).astype(jnp.int32) for m in range(1, SHARE))
    loose = jnp.where(q_e == r_e + (PAD - CAP) * group_e, 1.0, 0.0).astype(BF)

    channels = x_in.shape[1]
    tiles = channels // 128

    def tiled(ref, values):
        for j in range(tiles):
            ref[:, j, :] = values[:, j * 128:(j + 1) * 128]

    step = jax.nn.softplus(dot(dt_low[...], dt_weight[...]) + dt_bias[...])
    tiled(delta, step)
    tiled(rates, -jnp.exp(a_log[...]))

    mail = Mail(send, recv)
    pl.semaphore_wait(barrier, 16 + 3 + 7 + 1 - 2 * mine.astype(jnp.int32) + jnp.where(ends, 0, 1) + NZ - 1 - z)

    IN1, RT, RS, ACT, YC, YS, ZR = 0, 8, 18, 33, 53, 57, 61
    RET, LG, WG, WD, TAIL, ROW, ZALL, ENTRY = 62, 70, 78, 82, 83, 84, 88, 104

    for near_one, e, to in targets:
        mail.post(pack.at[e], in1.at[c, turn_j], IN1 + 4 * c + turn_j, to, mine if near_one else None)
    mail.post(x_in.at[pl.ds(tokens - 16, 16)], tail, TAIL, (seq + jnp.where(ends, 0, 1), exp), ends)
    own_group = z // 2
    stay = pltpu.make_async_copy(pack.at[own_group], in1.at[c, turn_j], local.at[NX + 1])
    pl.when(mine)(stay.start)
    for q in range(NX):
        mail.post(wg_in.at[:, pl.ds(q * ff, ff)], wg.at[c, q], WG + q, mate)
    mail.post(wd_in, wd.at[c], WD, mate)
    for j in range(1, 8):
        mail.post(lgs, lgr.at[exp], LG + exp, (seq, lax.rem(exp + j, 8)))
    mail.take(tail, TAIL, starts)
    before_rows = tail[...].astype(F32)[8:16]
    padded[0:8] = jnp.where(starts, 0.0, before_rows)
    padded[8:8 + tokens] = x_in[...].astype(F32)
    taps = conv_weight.shape[0]
    convolved = conv_bias[...]
    for k in range(taps):
        convolved = convolved + conv_weight[k:k + 1, :] * padded[9 - taps + k:9 - taps + k + tokens]
    activated = jax.nn.silu(convolved)
    active[...] = activated
    tiled(drive, step * activated)
    states = rates.shape[0]

    def own_step(t, carry):
        d, u = delta[t], drive[t]
        values = []
        for n in range(states):
            f = jnp.exp(d * rates[n])
            factor[t, n] = f
            values.append(f * carry[n] + b_and_c[0, n, t] * u)
        return tuple(values) + (carry[states] + d,)

    blank = jnp.zeros((tiles, 128), F32)
    final_state = lax.fori_loop(0, tokens, own_step, (blank,) * (states + 1))
    for n in range(states + 1):
        rowend[y, n] = final_state[n]
    for i, to_y in enumerate((near[1], near[-1], yfar)):
        mail.post(rowend.at[y], rowend.at[y], ROW + y, at(z, to_y, x, c))

    pl.when(mine)(stay.wait)
    for f, j, to in feeds:
        mail.take(in1.at[f, j], IN1 + 4 * f + j, is_me(f, j))
    feats = hid.shape[1]
    cols = [pl.ds(f * feats, feats) for f in range(2)]
    share = [half, 1 - half]
    for f in range(2):
        rt[0, half, :, cols[f]] = dot(tight, in1[f].reshape(SHARE * PAD, -1)).astype(BF)
    for w in share[:1]:
        mail.post(rt.at[0, w], rt.at[2, w], RT + 4 + w, ypeer[1])
        mail.post(rt.at[0, w], rt.at[1, w], RT + 2 + w, ypeer[-1])
        mail.post(rt.at[0, w], rt.at[0, w], RT + w, zpeer)
    quarter = states // NY
    for to_y in (near[1], near[-1], yfar):
        mail.take(rowend.at[to_y], ROW + to_y)
    ahead_sum, row_sum = blank, blank
    for other_y in range(NY):
        ahead_sum = jnp.where(y == other_y, row_sum, ahead_sum)
        row_sum = row_sum + rowend[other_y, states]
    for n in range(states):
        total, mine_before = blank, blank
        for other_y in range(NY):
            mine_before = jnp.where(y == other_y, total, mine_before)
            total = jnp.exp(rates[n] * rowend[other_y, states]) * total + rowend[other_y, n]
        state[n] = mine_before
        rowall[n // quarter, n % quarter] = total
    for i in range(NY):
        rowall[i, quarter] = row_sum
    for later in range(1, NZ):
        gone = z + later >= NZ
        mail.post(rowall.at[y], zall.at[z], ZALL + z, at(jnp.where(gone, z, z + later), y, x, c), gone)

    def along_z():
        def fold(other_z, carry):
            mail.take(zall.at[other_z], ZALL + other_z)
            decay = zall[other_z, quarter]
            return tuple(jnp.exp(rates[quarter * y + i] * decay) * carry[i] + zall[other_z, i]
                         for i in range(quarter))

        entering = lax.fori_loop(0, z, fold, (blank,) * quarter)
        for i in range(quarter):
            entry[y, i] = entering[i]
        for to_y in (near[1], near[-1], yfar):
            mail.post(entry.at[y], entry.at[y], ENTRY + y, at(z, to_y, x, c))

    def enter():
        for to_y in (near[1], near[-1], yfar):
            mail.take(entry.at[to_y], ENTRY + to_y)
        for n in range(states):
            state[n] = state[n] + jnp.exp(rates[n] * ahead_sum) * entry[n // quarter, n % quarter]

    pieces = 4

    def scan_piece(piece):
        def full_step(t, carry):
            u = drive[t]
            values, seen = [], None
            for n in range(states):
                value = factor[t, n] * carry[n] + b_and_c[0, n, t] * u
                values.append(value)
                term = b_and_c[1, n, t] * value
                seen = term if seen is None else seen + term
            reads[t] = seen
            return tuple(values)

        length = tokens // pieces
        done = lax.fori_loop(piece * length, (piece + 1) * length, full_step,
                             tuple(state[n] for n in range(states)))
        for n in range(states):
            state[n] = done[n]

    def finish_mixer():
        for j in range(tiles):
            cols = slice(j * 128, (j + 1) * 128)
            gate = jax.nn.silu(z_gate[:, cols].astype(F32))
            mixed[:, cols] = ((reads[:, j, :] + d_skip[:, cols] * active[:, cols]) * gate).astype(BF)

    for copy in loads:
        copy.wait()
    for q in range(NX):
        mail.take(wg.at[1 - c, q], WG + q)

    def gathered(k, i):
        w = share[i]
        if k == 0:
            mail.take(rt.at[0, w], RT + w)
            mail.post(rt.at[0, w], rt.at[2, w], RT + 4 + w, ypeer[1])
            mail.post(rt.at[0, w], rt.at[1, w], RT + 2 + w, ypeer[-1])
        elif k < 3:
            mail.take(rt.at[k, w], RT + 2 * k + w)
            f = k - 1 if k == 1 else 1
            mail.post(rt.at[k, w, :, cols[f]], rt.at[3, w, :, cols[f]], RT + 6 + 2 * w + f, ypeer[-1 if k == 1 else 1])
        else:
            for f in range(2):
                mail.take(rt.at[3, w, :, cols[f]], RT + 6 + 2 * w + f)

    def take_down():
        mail.take(wd.at[1 - c], WD)

    def part(b, i, q):
        k, w = BATCHES[b][i]
        held = rt.at[k, share[w]]
        return dot(held[:, cols[0]], wg[0, q]) + dot(held[:, cols[1]], wg[1, q])

    way = [1, -1, 1, -1, 1]

    def blocks(b):
        return range(len(BATCHES[b]))

    def span(b):
        return pl.ds(0, len(BATCHES[b]))

    def first(b):
        d, r = way[b], span(b)
        for i in blocks(b):
            sbuf[b, 0, i] = part(b, i, xs[2]).astype(BF)
        mail.post(sbuf.at[b, 0, r], rbuf.at[b, 0, r], RS + 3 * b, xpeer[d])
        for i in blocks(b):
            sbuf[b, 1, i] = part(b, i, xs[-d]).astype(BF)
        mail.post(sbuf.at[b, 1, r], rbuf.at[b, 1, r], RS + 3 * b + 1, xpeer[-d])
        for i in blocks(b):
            sbuf[b, 2, i] = part(b, i, xs[d]).astype(BF)
            sbuf[b, 3, i] = part(b, i, x).astype(BF)

    def second(b):
        d, r = way[b], span(b)
        mail.take(rbuf.at[b, 0, r], RS + 3 * b)
        for i in blocks(b):
            sbuf[b, 4, i] = (sbuf[b, 2, i].astype(F32) + rbuf[b, 0, i].astype(F32)).astype(BF)
        mail.post(sbuf.at[b, 4, r], rbuf.at[b, 2, r], RS + 3 * b + 2, xpeer[d])

    def third(b):
        r = span(b)
        mail.take(rbuf.at[b, 1, r], RS + 3 * b + 1)
        mail.take(rbuf.at[b, 2, r], RS + 3 * b + 2)
        for i in blocks(b):
            total = sbuf[b, 3, i].astype(F32) + rbuf[b, 1, i].astype(F32) + rbuf[b, 2, i].astype(F32)
            act[b, x, i] = jax.nn.silu(total).astype(BF)
        for d in (1, -1):
            mail.post(act.at[b, x, r], act.at[b, x, r], ACT + 4 * b + x, xpeer[d])

    def fourth(b):
        d, r = way[b], span(b)
        mail.take(act.at[b, xs[-d], r], ACT + 4 * b + xs[-d])
        mail.post(act.at[b, xs[-d], r], act.at[b, xs[-d], r], ACT + 4 * b + xs[-d], xpeer[d])

    def down(b):
        d, r = way[b], span(b)
        mail.take(act.at[b, xs[d], r], ACT + 4 * b + xs[d])
        mail.take(act.at[b, xs[2], r], ACT + 4 * b + xs[2])
        for i in blocks(b):
            k, w = BATCHES[b][i]
            for f in range(2):
                total = dot(act[b, 0, i], wd[f, 0:ff])
                for q in range(1, NX):
                    total += dot(act[b, q, i], wd[f, q * ff:(q + 1) * ff])
                prod[k, share[w], :, cols[f]] = total.astype(BF)

    def far(i):
        w = share[i]
        for f, d in ((0, 1), (1, -1)):
            mail.post(prod.at[3, w, :, cols[f]], yc.at[w, f], YC + 2 * w + f, ypeer[d])

    def combine(i):
        w = share[i]
        for f, d in ((0, 1), (1, -1)):
            mail.take(yc.at[w, f], YC + 2 * w + f)
            zs[w, f, :, cols[f]] = (prod[1 + f, w, :, cols[f]].astype(F32) + yc[w, f].astype(F32)).astype(BF)
            zs[w, f, :, cols[1 - f]] = prod[1 + f, w, :, cols[1 - f]]
            mail.post(zs.at[w, f], ys.at[w, f], YS + 2 * w + f, ypeer[d])

    steps = [
        (first, 0), (gathered, 1, 0), (gathered, 2, 0), (gathered, 0, 1), (first, 1), (second, 0), (gathered, 3, 0),
        (third, 0), (second, 1), (gathered, 1, 1), (gathered, 2, 1), (fourth, 0), (gathered, 3, 1), (first, 2),
        (third, 1), (first, 3), (second, 2), (fourth, 1), (take_down,), (down, 0), (first, 4), (second, 3), (third, 2),
        (down, 1), (along_z,), (second, 4), (fourth, 2), (third, 3), (down, 2), (far, 0), (far, 1), (third, 4),
        (fourth, 3), (combine, 0), (down, 3), (combine, 1), (fourth, 4), (down, 4)]
    for step_of, *which in steps:
        step_of(*which)

    def over_y(i):
        w = share[i]
        for f in range(2):
            mail.take(ys.at[w, f], YS + 2 * w + f)
        return prod[0, w].astype(F32) + ys[w, 0].astype(F32) + ys[w, 1].astype(F32)

    zb[...] = over_y(1).astype(BF)
    mail.post(zb, zr, ZR, zpeer)
    kept = over_y(0)
    mail.take(zr, ZR)
    whole = (kept + zr[...].astype(F32)).astype(BF)
    for f in range(2):
        back[f] = dot(loose, whole[:, f * feats:(f + 1) * feats]).astype(BF).reshape(back.shape[1:])
    for f, j, to in feeds:
        mail.post(back.at[f, j], ret.at[own_group], RET + own_group, to, is_me(f, j))
    last = pltpu.make_async_copy(back.at[c, turn_j], ret.at[own_group], local.at[NX + 2])
    pl.when(mine)(last.start)

    enter()
    for piece in range(pieces):
        scan_piece(piece)
    finish_mixer()
    for j in range(1, 8):
        q = lax.rem(exp + j, 8)
        mail.take(lgr.at[q], LG + q)
    lgr[exp] = lgs[...]
    logits = lgr[0]
    for q in range(1, 8):
        logits += lgr[q]
    logits = logits[:, :tokens]
    picked = [jnp.sum(hits[k] * logits, axis=0, keepdims=True) for k in range(2)]
    gates = [jax.nn.sigmoid(picked[0] - picked[1]), jax.nn.sigmoid(picked[1] - picked[0])]
    blend = jnp.where(match[0], gates[0], 0.0) + jnp.where(match[1], gates[1], 0.0)
    upper = blend.astype(BF)
    lower = (blend - upper.astype(F32)).astype(BF)

    pl.when(mine)(last.wait)
    for near_one, e, to in targets:
        mail.take(ret.at[e], RET + e, mine if near_one else None)
    rows_in = ret[...].reshape(experts * PAD, -1)
    turn = (((0,), (0,)), ((), ()))
    out[...] = (lax.dot_general(upper, rows_in, turn, preferred_element_type=F32)
                + lax.dot_general(lower, rows_in, turn, preferred_element_type=F32)).astype(BF)
    mail.finish()


def local(x_in, z_gate, dt_low, dt_weight, dt_bias, a_log, conv_weight, conv_bias, d_skip, b_and_c,
          hidden, router, expert_ids, w_gate, w_down):
    tokens, feats = hidden.shape
    channels, states = x_in.shape[1], a_log.shape[0]
    tiles, quarter = channels // 128, states // NY
    rows, ff = CAP * SHARE, w_gate.shape[1] // NX
    vm = pl.BlockSpec(memory_space=pltpu.VMEM)
    hbm = pl.BlockSpec(memory_space=pl.ANY)
    sm = pl.BlockSpec(memory_space=pltpu.SMEM)

    def row(a):
        return a.reshape(1, channels)

    return pl.pallas_call(
        layer_kernel,
        out_shape=(jax.ShapeDtypeStruct((tokens, channels), BF), jax.ShapeDtypeStruct((tokens, feats), BF)),
        in_specs=[vm] * 9 + [sm] + [vm] * 3 + [hbm] * 2,
        out_specs=(vm, vm),
        scratch_shapes=[
            pltpu.VMEM((2, NX, feats, ff), BF),
            pltpu.VMEM((2, NX * ff, feats), BF),
            pltpu.VMEM((8, PAD, feats), BF),
            pltpu.VMEM((2, SHARE, PAD, feats), BF),
            pltpu.VMEM((4, 2, rows, 2 * feats), BF),
            pltpu.VMEM((len(BATCHES), 5, 2, rows, ff), BF),
            pltpu.VMEM((len(BATCHES), 3, 2, rows, ff), BF),
            pltpu.VMEM((len(BATCHES), NX, 2, rows, ff), BF),
            pltpu.VMEM((4, 2, rows, 2 * feats), BF),
            pltpu.VMEM((2, 2, rows, 2 * feats), BF),
            pltpu.VMEM((2, 2, rows, feats), BF),
            pltpu.VMEM((2, 2, rows, 2 * feats), BF),
            pltpu.VMEM((rows, 2 * feats), BF),
            pltpu.VMEM((2, SHARE, PAD, feats), BF),
            pltpu.VMEM((8, PAD, feats), BF),
            pltpu.VMEM((8, 128), F32),
            pltpu.VMEM((8, 8, 128), F32),
            pltpu.VMEM((rows, 2 * feats), BF),
            pltpu.VMEM((16, channels), BF),
            pltpu.VMEM((8 + tokens, channels), F32),
            pltpu.VMEM((tokens, channels), F32),
            pltpu.VMEM((tokens, tiles, 128), F32),
            pltpu.VMEM((tokens, tiles, 128), F32),
            pltpu.VMEM((states, tiles, 128), F32),
            pltpu.VMEM((tokens, states, tiles, 128), F32),
            pltpu.VMEM((states, tiles, 128), F32),
            pltpu.VMEM((NY, states + 1, tiles, 128), F32),
            pltpu.VMEM((NY, quarter + 1, tiles, 128), F32),
            pltpu.VMEM((NZ, quarter + 1, tiles, 128), F32),
            pltpu.VMEM((NY, quarter, tiles, 128), F32),
            pltpu.VMEM((tokens, tiles, 128), F32),
            pltpu.SemaphoreType.DMA((128,)),
            pltpu.SemaphoreType.DMA((128,)),
            pltpu.SemaphoreType.DMA((8,)),
        ],
        compiler_params=pltpu.CompilerParams(collective_id=0, has_side_effects=True,
                                             vmem_limit_bytes=60 * 1024 * 1024),
        name="layer",
    )(x_in, z_gate, dt_low, dt_weight, row(dt_bias), a_log, conv_weight, row(conv_bias), row(d_skip), b_and_c,
      hidden, router.T, expert_ids.T, w_gate, w_down)


def solution(mesh):
    return jax.shard_map(
        local,
        mesh=mesh,
        in_specs=(
            P("seq", "exp"),
            P("seq", "exp"),
            P("seq", None),
            P(None, "exp"),
            P("exp"),
            P(None, "exp"),
            P(None, "exp"),
            P("exp"),
            P("exp"),
            P(None, None, "seq"),
            P("seq", "exp"),
            P("exp", None),
            P("seq", None),
            P("exp", "seq"),
            P("seq", "exp"),
        ),
        out_specs=(P("seq", "exp"), P("seq", "exp")),
        check_vma=False,
    )
```

```python
import functools

import jax
import jax.numpy as jnp
from jax import lax
from jax.experimental import pallas as pl
from jax.experimental.pallas import tpu as pltpu
from jax.sharding import PartitionSpec as P

CAP = 18
PAD = 24
NZ, NY, NX = 16, 4, 4
DIRECT = 4
MESH = pl.DeviceIdType.MESH
BF, F32 = jnp.bfloat16, jnp.float32
SHARE = 4
BATCHES = (((0, 0),), ((1, 0), (2, 0)), ((3, 0), (3, 1)), ((1, 1), (2, 1)), ((0, 1),))


def dot(a, b):
    return jnp.dot(a, b, preferred_element_type=F32)


class Mail:
    def __init__(self, send, recv):
        self.send, self.recv, self.count, self.sent = send, recv, 0, []

    def post(self, src, dst, slot, to, unless=None):
        copy = pltpu.make_async_remote_copy(
            src_ref=src, dst_ref=dst, send_sem=self.send.at[self.count], recv_sem=self.recv.at[slot],
            device_id=to, device_id_type=MESH)
        self.count += 1
        self.sent.append((copy, unless))
        if unless is None:
            copy.start()
        else:
            pl.when(jnp.logical_not(unless))(copy.start)

    def take(self, dst, slot, unless=None):
        copy = pltpu.make_async_remote_copy(
            src_ref=dst, dst_ref=dst, send_sem=self.send.at[0], recv_sem=self.recv.at[slot],
            device_id=(lax.axis_index("seq"), lax.axis_index("exp")), device_id_type=MESH)
        if unless is None:
            copy.wait_recv()
        else:
            pl.when(jnp.logical_not(unless))(copy.wait_recv)

    def finish(self):
        for copy, unless in self.sent:
            if unless is None:
                copy.wait_send()
            else:
                pl.when(jnp.logical_not(unless))(copy.wait_send)


def layer_kernel(x_in_hbm, z_gate_hbm, dt_low_hbm, dt_weight_hbm, dt_bias_hbm, a_log_hbm, conv_weight_hbm, conv_bias_hbm,
                 d_skip_hbm, b_and_c, hid_hbm, router_t_hbm, ids_t, wg_in, wd_in, mixed, out, wg, wd, pack,
                 in1, rt, sbuf, rbuf, act, prod, ys, yc, zs, zr, back, ret, lgs, lgr, zb, prior, tail, padded,
                 active, delta, drive, rates, factor, state, rowend, rowall, zall, entry, reads, send, recv,
                 local, intake, x_in, z_gate, dt_low, dt_weight, dt_bias, a_log, conv_weight, conv_bias,
                 d_skip, hid, router_t):
    seq, exp = lax.axis_index("seq"), lax.axis_index("exp")
    z, y, x, c = seq // NY, lax.rem(seq, NY), exp // 2, lax.rem(exp, 2)
    half = lax.rem(z, 2)
    zpair = z + 1 - 2 * half
    near = {1: lax.rem(y + 1, NY), -1: lax.rem(y + NY - 1, NY)}
    xs = {d: lax.rem(x + d + NX, NX) for d in (-1, 0, 1, 2)}
    ff = wg.shape[3]

    def at(z_, y_, x_, c_):
        return (z_ * NY + y_, x_ * 2 + c_)

    mate = at(z, y, x, 1 - c)
    ypeer = {d: at(z, near[d], x, c) for d in (1, -1)}
    xpeer = {d: at(z, y, xs[d], c) for d in (1, -1)}
    zpeer = at(zpair, y, x, c)
    xfar = at(z, y, xs[2], c)
    experts = 8

    barrier = pltpu.get_barrier_semaphore()

    def greet(to):
        pl.semaphore_signal(barrier, inc=1, device_id=to, device_id_type=MESH)

    def unless(cond, work):
        pl.when(jnp.logical_not(cond))(work)

    order = [4, 3, 5, 2, 6, 1, 7, 0]
    groups = [lax.rem(z // 2 + off, experts) for off in order]
    wide, turn_j = lax.rem(z // 2, 2), z // 4
    mine = (half == c) & (wide == half)
    targets = [(off == 0, e, at(2 * e + wide, y, x, half)) for off, e in zip(order, groups)]
    feeds = [(f, j, at(4 * j + 2 * half + c, y, x, f)) for j in range(SHARE) for f in range(2)]

    def is_me(f, j):
        return mine & (c == f) & (turn_j == j)

    for near_one, e, to in targets:
        if near_one:
            unless(mine, functools.partial(greet, to))
        else:
            greet(to)
    for f, j, to in feeds:
        unless(is_me(f, j), functools.partial(greet, to))
    for to in (zpeer, ypeer[1], ypeer[-1]):
        greet(to)
    for j in range(1, 8):
        greet((seq, lax.rem(exp + j, 8)))
    yfar = lax.rem(y + 2, NY)
    greet(at(z, yfar, x, c))
    starts, ends = seq == 0, seq == NZ * NY - 1
    pl.when(jnp.logical_not(starts))(functools.partial(greet, (seq - jnp.where(starts, 0, 1), exp)))

    def greet_earlier(other_z, carry):
        greet(at(other_z, y, x, c))
        return carry

    lax.fori_loop(0, z, greet_earlier, 0)

    staged = {}
    for n, (source, target) in enumerate((
            (hid_hbm, hid), (router_t_hbm, router_t), (x_in_hbm, x_in),
            (z_gate_hbm, z_gate),
            (dt_low_hbm, dt_low),
            (dt_weight_hbm, dt_weight),
            (dt_bias_hbm, dt_bias),
            (a_log_hbm, a_log),
            (conv_weight_hbm, conv_weight),
            (conv_bias_hbm, conv_bias),
            (d_skip_hbm, d_skip))):
        staged[n] = pltpu.make_async_copy(source, target, intake.at[n])
        staged[n].start()
    loads = []
    for q in range(NX):
        loads.append(pltpu.make_async_copy(wg_in.at[:, pl.ds(q * ff, ff)], wg.at[c, q], local.at[q]))
    loads.append(pltpu.make_async_copy(wd_in, wd.at[c], local.at[NX]))
    for copy in loads:
        copy.start()

    for n in (0, 1):
        staged[n].wait()
    ids = ids_t[...]
    tokens = ids.shape[1]
    e_iota = lax.broadcasted_iota(jnp.int32, (experts, tokens), 0)
    hits = [(ids[k:k + 1, :] == e_iota).astype(F32) for k in range(2)]
    ahead = (lax.broadcasted_iota(jnp.int32, (tokens, tokens), 0)
             < lax.broadcasted_iota(jnp.int32, (tokens, tokens), 1)).astype(BF)
    before = dot((hits[0] + hits[1]).astype(BF), ahead)
    keys = [ids[k:k + 1, :] * PAD + jnp.sum(hits[k] * before, axis=0, keepdims=True).astype(jnp.int32)
            for k in range(2)]
    r_iota = lax.broadcasted_iota(jnp.int32, (experts * PAD, tokens), 0)
    match = [r_iota == keys[k] for k in range(2)]
    selector = jnp.where(match[0] | match[1], 1.0, 0.0).astype(BF)
    h = hid[...]
    pack[...] = dot(selector, h).astype(BF).reshape(pack.shape)
    lg = lax.dot_general(router_t[...], h, (((1,), (1,)), ((), ())), preferred_element_type=F32)
    lgs[...] = jnp.concatenate([lg, jnp.zeros((experts, 128 - tokens), F32)], axis=1)
    rows = CAP * SHARE
    r_c = lax.broadcasted_iota(jnp.int32, (rows, SHARE * PAD), 0)
    q_c = lax.broadcasted_iota(jnp.int32, (rows, SHARE * PAD), 1)
    group = sum((r_c >= CAP * m).astype(jnp.int32) for m in range(1, SHARE))
    tight = jnp.where(q_c == r_c + (PAD - CAP) * group, 1.0, 0.0).astype(BF)
    q_e = lax.broadcasted_iota(jnp.int32, (SHARE * PAD, rows), 0)
    r_e = lax.broadcasted_iota(jnp.int32, (SHARE * PAD, rows), 1)
    group_e = sum((r_e >= CAP * m).astype(jnp.int32) for m in range(1, SHARE))
    loose = jnp.where(q_e == r_e + (PAD - CAP) * group_e, 1.0, 0.0).astype(BF)

    for n in range(2, len(staged)):
        staged[n].wait()
    channels = x_in.shape[1]
    tiles = channels // 128

    def tiled(ref, values):
        for j in range(tiles):
            ref[:, j, :] = values[:, j * 128:(j + 1) * 128]

    step = jax.nn.softplus(dot(dt_low[...], dt_weight[...]) + dt_bias[...])
    tiled(delta, step)
    tiled(rates, -jnp.exp(a_log[...]))

    mail = Mail(send, recv)
    pl.semaphore_wait(barrier, 16 + 3 + 7 + 1 - 2 * mine.astype(jnp.int32) + jnp.where(ends, 0, 1) + NZ - 1 - z)

    IN1, RT, RS, ACT, YC, YS, ZR = 0, 8, 18, 33, 53, 57, 61
    RET, LG, WG, WD, TAIL, ROW, ZALL, ENTRY = 62, 70, 78, 82, 83, 84, 88, 104

    for near_one, e, to in targets:
        mail.post(pack.at[e], in1.at[c, turn_j], IN1 + 4 * c + turn_j, to, mine if near_one else None)
    mail.post(x_in.at[pl.ds(tokens - 16, 16)], tail, TAIL, (seq + jnp.where(ends, 0, 1), exp), ends)
    own_group = z // 2
    stay = pltpu.make_async_copy(pack.at[own_group], in1.at[c, turn_j], local.at[NX + 1])
    pl.when(mine)(stay.start)
    for q in range(NX):
        mail.post(wg_in.at[:, pl.ds(q * ff, ff)], wg.at[c, q], WG + q, mate)
    mail.post(wd_in, wd.at[c], WD, mate)
    for j in range(1, 8):
        mail.post(lgs, lgr.at[exp], LG + exp, (seq, lax.rem(exp + j, 8)))
    mail.take(tail, TAIL, starts)
    before_rows = tail[...].astype(F32)[8:16]
    padded[0:8] = jnp.where(starts, 0.0, before_rows)
    padded[8:8 + tokens] = x_in[...].astype(F32)
    taps = conv_weight.shape[0]
    convolved = conv_bias[...]
    for k in range(taps):
        convolved = convolved + conv_weight[k:k + 1, :] * padded[9 - taps + k:9 - taps + k + tokens]
    activated = jax.nn.silu(convolved)
    active[...] = activated
    tiled(drive, step * activated)
    states = rates.shape[0]

    def own_step(t, carry):
        d, u = delta[t], drive[t]
        values = []
        for n in range(states):
            f = jnp.exp(d * rates[n])
            factor[t, n] = f
            values.append(f * carry[n] + b_and_c[0, n, t] * u)
        return tuple(values) + (carry[states] + d,)

    blank = jnp.zeros((tiles, 128), F32)
    final_state = lax.fori_loop(0, tokens, own_step, (blank,) * (states + 1))
    for n in range(states + 1):
        rowend[y, n] = final_state[n]
    for i, to_y in enumerate((near[1], near[-1], yfar)):
        mail.post(rowend.at[y], rowend.at[y], ROW + y, at(z, to_y, x, c))

    pl.when(mine)(stay.wait)
    for f, j, to in feeds:
        mail.take(in1.at[f, j], IN1 + 4 * f + j, is_me(f, j))
    feats = hid.shape[1]
    cols = [pl.ds(f * feats, feats) for f in range(2)]
    share = [half, 1 - half]
    for f in range(2):
        rt[0, half, :, cols[f]] = dot(tight, in1[f].reshape(SHARE * PAD, -1)).astype(BF)
    for w in share[:1]:
        mail.post(rt.at[0, w], rt.at[2, w], RT + 4 + w, ypeer[1])
        mail.post(rt.at[0, w], rt.at[1, w], RT + 2 + w, ypeer[-1])
        mail.post(rt.at[0, w], rt.at[0, w], RT + w, zpeer)
    quarter = states // NY

    def along_y():
        for to_y in (near[1], near[-1], yfar):
            mail.take(rowend.at[to_y], ROW + to_y)
        ahead_sum, row_sum = blank, blank
        for other_y in range(NY):
            ahead_sum = jnp.where(y == other_y, row_sum, ahead_sum)
            row_sum = row_sum + rowend[other_y, states]
        for n in range(states):
            total, mine_before = blank, blank
            for other_y in range(NY):
                mine_before = jnp.where(y == other_y, total, mine_before)
                total = jnp.exp(rates[n] * rowend[other_y, states]) * total + rowend[other_y, n]
            state[n] = mine_before
            rowall[n // quarter, n % quarter] = total
        for i in range(NY):
            rowall[i, quarter] = row_sum
        for later in range(1, NZ):
            gone = z + later >= NZ
            mail.post(rowall.at[y], zall.at[z], ZALL + z, at(jnp.where(gone, z, z + later), y, x, c), gone)
        prior[...] = ahead_sum

    def along_z():
        def fold(other_z, carry):
            mail.take(zall.at[other_z], ZALL + other_z)
            decay = zall[other_z, quarter]
            return tuple(jnp.exp(rates[quarter * y + i] * decay) * carry[i] + zall[other_z, i]
                         for i in range(quarter))

        entering = lax.fori_loop(0, z, fold, (blank,) * quarter)
        for i in range(quarter):
            entry[y, i] = entering[i]
        for to_y in (near[1], near[-1], yfar):
            mail.post(entry.at[y], entry.at[y], ENTRY + y, at(z, to_y, x, c))

    def enter():
        for to_y in (near[1], near[-1], yfar):
            mail.take(entry.at[to_y], ENTRY + to_y)
        for n in range(states):
            state[n] = state[n] + jnp.exp(rates[n] * prior[...]) * entry[n // quarter, n % quarter]

    pieces = 4

    def scan_piece(piece):
        def full_step(t, carry):
            u = drive[t]
            values, seen = [], None
            for n in range(states):
                value = factor[t, n] * carry[n] + b_and_c[0, n, t] * u
                values.append(value)
                term = b_and_c[1, n, t] * value
                seen = term if seen is None else seen + term
            reads[t] = seen
            return tuple(values)

        length = tokens // pieces
        done = lax.fori_loop(piece * length, (piece + 1) * length, full_step,
                             tuple(state[n] for n in range(states)))
        for n in range(states):
            state[n] = done[n]

    def finish_mixer():
        for j in range(tiles):
            cols = slice(j * 128, (j + 1) * 128)
            gate = jax.nn.silu(z_gate[:, cols].astype(F32))
            mixed[:, cols] = ((reads[:, j, :] + d_skip[:, cols] * active[:, cols]) * gate).astype(BF)

    for copy in loads:
        copy.wait()
    for q in range(NX):
        mail.take(wg.at[1 - c, q], WG + q)

    def gathered(k, i):
        w = share[i]
        if k == 0:
            mail.take(rt.at[0, w], RT + w)
            mail.post(rt.at[0, w], rt.at[2, w], RT + 4 + w, ypeer[1])
            mail.post(rt.at[0, w], rt.at[1, w], RT + 2 + w, ypeer[-1])
        elif k < 3:
            mail.take(rt.at[k, w], RT + 2 * k + w)
            f = k - 1 if k == 1 else 1
            mail.post(rt.at[k, w, :, cols[f]], rt.at[3, w, :, cols[f]], RT + 6 + 2 * w + f, ypeer[-1 if k == 1 else 1])
        else:
            for f in range(2):
                mail.take(rt.at[3, w, :, cols[f]], RT + 6 + 2 * w + f)

    def take_down():
        mail.take(wd.at[1 - c], WD)

    def part(b, i, q):
        k, w = BATCHES[b][i]
        held = rt.at[k, share[w]]
        return dot(held[:, cols[0]], wg[0, q]) + dot(held[:, cols[1]], wg[1, q])

    way = [1, -1, 1, -1, 1]

    def blocks(b):
        return range(len(BATCHES[b]))

    def span(b):
        return pl.ds(0, len(BATCHES[b]))

    def first(b):
        d, r = way[b], span(b)
        for i in blocks(b):
            sbuf[b, 0, i] = part(b, i, xs[2]).astype(BF)
        mail.post(sbuf.at[b, 0, r], rbuf.at[b, 0, r], RS + 3 * b, xfar if b == DIRECT else xpeer[d])
        if b == DIRECT:
            for slot, way_to in ((1, -d), (2, d)):
                for i in blocks(b):
                    sbuf[b, slot, i] = part(b, i, xs[way_to]).astype(BF)
                mail.post(sbuf.at[b, slot, r], rbuf.at[b, slot, r], RS + 3 * b + slot, xpeer[way_to])
            for i in blocks(b):
                sbuf[b, 3, i] = part(b, i, x).astype(BF)
            return
        for i in blocks(b):
            sbuf[b, 1, i] = part(b, i, xs[-d]).astype(BF)
        mail.post(sbuf.at[b, 1, r], rbuf.at[b, 1, r], RS + 3 * b + 1, xpeer[-d])
        for i in blocks(b):
            sbuf[b, 2, i] = part(b, i, xs[d]).astype(BF)
            sbuf[b, 3, i] = part(b, i, x).astype(BF)

    def second(b):
        d, r = way[b], span(b)
        mail.take(rbuf.at[b, 0, r], RS + 3 * b)
        for i in blocks(b):
            sbuf[b, 4, i] = (sbuf[b, 2, i].astype(F32) + rbuf[b, 0, i].astype(F32)).astype(BF)
        mail.post(sbuf.at[b, 4, r], rbuf.at[b, 2, r], RS + 3 * b + 2, xpeer[d])

    def third(b):
        r = span(b)
        if b == DIRECT:
            mail.take(rbuf.at[b, 0, r], RS + 3 * b)
        mail.take(rbuf.at[b, 1, r], RS + 3 * b + 1)
        mail.take(rbuf.at[b, 2, r], RS + 3 * b + 2)
        for i in blocks(b):
            total = sbuf[b, 3, i].astype(F32) + rbuf[b, 1, i].astype(F32) + rbuf[b, 2, i].astype(F32)
            if b == DIRECT:
                total += rbuf[b, 0, i].astype(F32)
            act[b, x, i] = jax.nn.silu(total).astype(BF)
        for to in (xpeer[1], xpeer[-1]) + ((xfar,) if b == DIRECT else ()):
            mail.post(act.at[b, x, r], act.at[b, x, r], ACT + 4 * b + x, to)

    def fourth(b):
        d, r = way[b], span(b)
        mail.take(act.at[b, xs[-d], r], ACT + 4 * b + xs[-d])
        mail.post(act.at[b, xs[-d], r], act.at[b, xs[-d], r], ACT + 4 * b + xs[-d], xpeer[d])

    def down(b):
        d, r = way[b], span(b)
        mail.take(act.at[b, xs[d], r], ACT + 4 * b + xs[d])
        if b == DIRECT:
            mail.take(act.at[b, xs[-d], r], ACT + 4 * b + xs[-d])
        mail.take(act.at[b, xs[2], r], ACT + 4 * b + xs[2])
        for i in blocks(b):
            k, w = BATCHES[b][i]
            for f in range(2):
                total = dot(act[b, 0, i], wd[f, 0:ff])
                for q in range(1, NX):
                    total += dot(act[b, q, i], wd[f, q * ff:(q + 1) * ff])
                prod[k, share[w], :, cols[f]] = total.astype(BF)

    def far(i):
        w = share[i]
        for f, d in ((0, 1), (1, -1)):
            mail.post(prod.at[3, w, :, cols[f]], yc.at[w, f], YC + 2 * w + f, ypeer[d])

    def combine(i):
        w = share[i]
        for f, d in ((0, 1), (1, -1)):
            mail.take(yc.at[w, f], YC + 2 * w + f)
            zs[w, f, :, cols[f]] = (prod[1 + f, w, :, cols[f]].astype(F32) + yc[w, f].astype(F32)).astype(BF)
            zs[w, f, :, cols[1 - f]] = prod[1 + f, w, :, cols[1 - f]]
            mail.post(zs.at[w, f], ys.at[w, f], YS + 2 * w + f, ypeer[d])

    steps = [
        (first, 0), (gathered, 1, 0), (gathered, 2, 0), (gathered, 0, 1), (first, 1), (second, 0), (gathered, 3, 0),
        (third, 0), (second, 1), (gathered, 1, 1), (gathered, 2, 1), (fourth, 0), (gathered, 3, 1), (first, 2),
        (third, 1), (first, 3), (along_y,), (second, 2), (fourth, 1), (take_down,), (down, 0), (first, 4), (second, 3), (third, 2),
        (down, 1), (fourth, 2), (third, 3), (down, 2), (far, 0), (far, 1), (along_z,), (third, 4),
        (fourth, 3), (combine, 0), (down, 3), (combine, 1), (down, 4)]
    for step_of, *which in steps:
        step_of(*which)

    def over_y(i):
        w = share[i]
        for f in range(2):
            mail.take(ys.at[w, f], YS + 2 * w + f)
        return prod[0, w].astype(F32) + ys[w, 0].astype(F32) + ys[w, 1].astype(F32)

    passed, kept = over_y(1), None
    for f in range(2):
        zb[f] = passed[:, f * feats:(f + 1) * feats].astype(BF)
        mail.post(zb.at[f], zr.at[f], ZR + 47 * f, zpeer)
    kept = over_y(0)
    for f in range(2):
        mail.take(zr.at[f], ZR + 47 * f)
        whole = (kept[:, f * feats:(f + 1) * feats] + zr[f].astype(F32)).astype(BF)
        back[f] = dot(loose, whole).astype(BF).reshape(back.shape[1:])
        for g, j, to in feeds:
            if g == f:
                mail.post(back.at[f, j], ret.at[own_group], RET + own_group, to, is_me(f, j))
    last = pltpu.make_async_copy(back.at[c, turn_j], ret.at[own_group], local.at[NX + 2])
    pl.when(mine)(last.start)

    enter()
    for piece in range(pieces):
        scan_piece(piece)
    finish_mixer()
    for j in range(1, 8):
        q = lax.rem(exp + j, 8)
        mail.take(lgr.at[q], LG + q)
    lgr[exp] = lgs[...]
    logits = lgr[0]
    for q in range(1, 8):
        logits += lgr[q]
    logits = logits[:, :tokens]
    picked = [jnp.sum(hits[k] * logits, axis=0, keepdims=True) for k in range(2)]
    gates = [jax.nn.sigmoid(picked[0] - picked[1]), jax.nn.sigmoid(picked[1] - picked[0])]
    blend = jnp.where(match[0], gates[0], 0.0) + jnp.where(match[1], gates[1], 0.0)
    upper = blend.astype(BF)
    lower = (blend - upper.astype(F32)).astype(BF)

    pl.when(mine)(last.wait)
    for near_one, e, to in targets:
        mail.take(ret.at[e], RET + e, mine if near_one else None)
    rows_in = ret[...].reshape(experts * PAD, -1)
    turn = (((0,), (0,)), ((), ()))
    out[...] = (lax.dot_general(upper, rows_in, turn, preferred_element_type=F32)
                + lax.dot_general(lower, rows_in, turn, preferred_element_type=F32)).astype(BF)
    mail.finish()


def local(x_in, z_gate, dt_low, dt_weight, dt_bias, a_log, conv_weight, conv_bias, d_skip, b_and_c,
          hidden, router, expert_ids, w_gate, w_down):
    tokens, feats = hidden.shape
    channels, states = x_in.shape[1], a_log.shape[0]
    tiles, quarter = channels // 128, states // NY
    rows, ff = CAP * SHARE, w_gate.shape[1] // NX
    vm = pl.BlockSpec(memory_space=pltpu.VMEM)
    hbm = pl.BlockSpec(memory_space=pl.ANY)
    sm = pl.BlockSpec(memory_space=pltpu.SMEM)

    def row(a):
        return a.reshape(1, channels)

    return pl.pallas_call(
        layer_kernel,
        out_shape=(jax.ShapeDtypeStruct((tokens, channels), BF), jax.ShapeDtypeStruct((tokens, feats), BF)),
        in_specs=[hbm] * 9 + [sm] + [hbm] * 2 + [vm] + [hbm] * 2,
        out_specs=(vm, vm),
        scratch_shapes=[
            pltpu.VMEM((2, NX, feats, ff), BF),
            pltpu.VMEM((2, NX * ff, feats), BF),
            pltpu.VMEM((8, PAD, feats), BF),
            pltpu.VMEM((2, SHARE, PAD, feats), BF),
            pltpu.VMEM((4, 2, rows, 2 * feats), BF),
            pltpu.VMEM((len(BATCHES), 5, 2, rows, ff), BF),
            pltpu.VMEM((len(BATCHES), 3, 2, rows, ff), BF),
            pltpu.VMEM((len(BATCHES), NX, 2, rows, ff), BF),
            pltpu.VMEM((4, 2, rows, 2 * feats), BF),
            pltpu.VMEM((2, 2, rows, 2 * feats), BF),
            pltpu.VMEM((2, 2, rows, feats), BF),
            pltpu.VMEM((2, 2, rows, 2 * feats), BF),
            pltpu.VMEM((2, rows, feats), BF),
            pltpu.VMEM((2, SHARE, PAD, feats), BF),
            pltpu.VMEM((8, PAD, feats), BF),
            pltpu.VMEM((8, 128), F32),
            pltpu.VMEM((8, 8, 128), F32),
            pltpu.VMEM((2, rows, feats), BF),
            pltpu.VMEM((tiles, 128), F32),
            pltpu.VMEM((16, channels), BF),
            pltpu.VMEM((8 + tokens, channels), F32),
            pltpu.VMEM((tokens, channels), F32),
            pltpu.VMEM((tokens, tiles, 128), F32),
            pltpu.VMEM((tokens, tiles, 128), F32),
            pltpu.VMEM((states, tiles, 128), F32),
            pltpu.VMEM((tokens, states, tiles, 128), F32),
            pltpu.VMEM((states, tiles, 128), F32),
            pltpu.VMEM((NY, states + 1, tiles, 128), F32),
            pltpu.VMEM((NY, quarter + 1, tiles, 128), F32),
            pltpu.VMEM((NZ, quarter + 1, tiles, 128), F32),
            pltpu.VMEM((NY, quarter, tiles, 128), F32),
            pltpu.VMEM((tokens, tiles, 128), F32),
            pltpu.SemaphoreType.DMA((128,)),
            pltpu.SemaphoreType.DMA((128,)),
            pltpu.SemaphoreType.DMA((8,)),
            pltpu.SemaphoreType.DMA((16,)),
            pltpu.VMEM((tokens, channels), BF),
            pltpu.VMEM((tokens, channels), BF),
            pltpu.VMEM(dt_low.shape, BF),
            pltpu.VMEM(dt_weight.shape, BF),
            pltpu.VMEM((1, channels), F32),
            pltpu.VMEM(a_log.shape, F32),
            pltpu.VMEM(conv_weight.shape, F32),
            pltpu.VMEM((1, channels), F32),
            pltpu.VMEM((1, channels), F32),
            pltpu.VMEM(hidden.shape, BF),
            pltpu.VMEM(router.shape[::-1], BF),
        ],
        compiler_params=pltpu.CompilerParams(collective_id=0, has_side_effects=True,
                                             vmem_limit_bytes=60 * 1024 * 1024),
        name="layer",
    )(x_in, z_gate, dt_low, dt_weight, row(dt_bias), a_log, conv_weight, row(conv_bias), row(d_skip), b_and_c,
      hidden, router.T, expert_ids.T, w_gate, w_down)


def solution(mesh):
    return jax.shard_map(
        local,
        mesh=mesh,
        in_specs=(
            P("seq", "exp"),
            P("seq", "exp"),
            P("seq", None),
            P(None, "exp"),
            P("exp"),
            P(None, "exp"),
            P(None, "exp"),
            P("exp"),
            P("exp"),
            P(None, None, "seq"),
            P("seq", "exp"),
            P("exp", None),
            P("seq", None),
            P("exp", "seq"),
            P("seq", "exp"),
        ),
        out_specs=(P("seq", "exp"), P("seq", "exp")),
        check_vma=False,
    )
```

```python
import functools

import jax
import jax.numpy as jnp
from jax import lax
from jax.experimental import pallas as pl
from jax.experimental.pallas import tpu as pltpu
from jax.sharding import PartitionSpec as P

CAP = 18
PAD = 24
NZ, NY, NX = 16, 4, 4
DIRECT = 4
MESH = pl.DeviceIdType.MESH
BF, F32 = jnp.bfloat16, jnp.float32
SHARE = 4
BATCHES = (((0, 0),), ((1, 0), (2, 0)), ((3, 0), (3, 1)), ((1, 1), (2, 1)), ((0, 1),))


def dot(a, b):
    return jnp.dot(a, b, preferred_element_type=F32)


class Mail:
    def __init__(self, send, recv):
        self.send, self.recv, self.count, self.sent = send, recv, 0, []

    def post(self, src, dst, slot, to, unless=None):
        copy = pltpu.make_async_remote_copy(
            src_ref=src, dst_ref=dst, send_sem=self.send.at[self.count], recv_sem=self.recv.at[slot],
            device_id=to, device_id_type=MESH)
        self.count += 1
        self.sent.append((copy, unless))
        if unless is None:
            copy.start()
        else:
            pl.when(jnp.logical_not(unless))(copy.start)

    def take(self, dst, slot, unless=None):
        copy = pltpu.make_async_remote_copy(
            src_ref=dst, dst_ref=dst, send_sem=self.send.at[0], recv_sem=self.recv.at[slot],
            device_id=(lax.axis_index("seq"), lax.axis_index("exp")), device_id_type=MESH)
        if unless is None:
            copy.wait_recv()
        else:
            pl.when(jnp.logical_not(unless))(copy.wait_recv)

    def finish(self):
        for copy, unless in self.sent:
            if unless is None:
                copy.wait_send()
            else:
                pl.when(jnp.logical_not(unless))(copy.wait_send)


def layer_kernel(x_in_hbm, z_gate_hbm, dt_low_hbm, dt_weight_hbm, dt_bias_hbm, a_log_hbm, conv_weight_hbm, conv_bias_hbm,
                 d_skip_hbm, b_and_c, hid_hbm, router_t_hbm, ids_t, wg_in, wd_in, mixed, out, wg, wd, pack,
                 in1, rt, sbuf, rbuf, act, prod, ys, yc, zs, zr, back, ret, lgs, lgr, zb, prior, tail, padded,
                 active, delta, drive, rates, factor, state, rowend, rowall, zall, entry, reads, send, recv,
                 local, intake, x_in, z_gate, dt_low, dt_weight, dt_bias, a_log, conv_weight, conv_bias,
                 d_skip, hid, router_t):
    seq, exp = lax.axis_index("seq"), lax.axis_index("exp")
    z, y, x, c = seq // NY, lax.rem(seq, NY), exp // 2, lax.rem(exp, 2)
    half = lax.rem(z, 2)
    zpair = z + 1 - 2 * half
    near = {1: lax.rem(y + 1, NY), -1: lax.rem(y + NY - 1, NY)}
    xs = {d: lax.rem(x + d + NX, NX) for d in (-1, 0, 1, 2)}
    ff = wg.shape[3]

    def at(z_, y_, x_, c_):
        return (z_ * NY + y_, x_ * 2 + c_)

    mate = at(z, y, x, 1 - c)
    ypeer = {d: at(z, near[d], x, c) for d in (1, -1)}
    xpeer = {d: at(z, y, xs[d], c) for d in (1, -1)}
    zpeer = at(zpair, y, x, c)
    xfar = at(z, y, xs[2], c)
    experts = 8

    barrier = pltpu.get_barrier_semaphore()

    def greet(to):
        pl.semaphore_signal(barrier, inc=1, device_id=to, device_id_type=MESH)

    def unless(cond, work):
        pl.when(jnp.logical_not(cond))(work)

    order = [4, 3, 5, 2, 6, 1, 7, 0]
    groups = [lax.rem(z // 2 + off, experts) for off in order]
    wide, turn_j = lax.rem(z // 2, 2), z // 4
    mine = (half == c) & (wide == half)
    targets = [(off == 0, e, at(2 * e + wide, y, x, half)) for off, e in zip(order, groups)]
    feeds = [(f, j, at(4 * j + 2 * half + c, y, x, f)) for j in range(SHARE) for f in range(2)]

    def is_me(f, j):
        return mine & (c == f) & (turn_j == j)

    for near_one, e, to in targets:
        if near_one:
            unless(mine, functools.partial(greet, to))
        else:
            greet(to)
    for f, j, to in feeds:
        unless(is_me(f, j), functools.partial(greet, to))
    for to in (zpeer, ypeer[1], ypeer[-1]):
        greet(to)
    for j in range(1, 8):
        greet((seq, lax.rem(exp + j, 8)))
    yfar = lax.rem(y + 2, NY)
    greet(at(z, yfar, x, c))
    starts, ends = seq == 0, seq == NZ * NY - 1
    pl.when(jnp.logical_not(starts))(functools.partial(greet, (seq - jnp.where(starts, 0, 1), exp)))

    def greet_earlier(other_z, carry):
        greet(at(other_z, y, x, c))
        return carry

    lax.fori_loop(0, z, greet_earlier, 0)

    staged = {}
    for n, (source, target) in enumerate((
            (hid_hbm, hid), (router_t_hbm, router_t), (x_in_hbm, x_in),
            (z_gate_hbm, z_gate),
            (dt_low_hbm, dt_low),
            (dt_weight_hbm, dt_weight),
            (dt_bias_hbm, dt_bias),
            (a_log_hbm, a_log),
            (conv_weight_hbm, conv_weight),
            (conv_bias_hbm, conv_bias),
            (d_skip_hbm, d_skip))):
        staged[n] = pltpu.make_async_copy(source, target, intake.at[n])
        staged[n].start()
    loads = []
    for q in range(NX):
        loads.append(pltpu.make_async_copy(wg_in.at[:, pl.ds(q * ff, ff)], wg.at[c, q], local.at[q]))
    loads.append(pltpu.make_async_copy(wd_in, wd.at[c], local.at[NX]))
    for copy in loads:
        copy.start()

    for n in (0, 1):
        staged[n].wait()
    ids = ids_t[...]
    tokens = ids.shape[1]
    e_iota = lax.broadcasted_iota(jnp.int32, (experts, tokens), 0)
    hits = [(ids[k:k + 1, :] == e_iota).astype(F32) for k in range(2)]
    ahead = (lax.broadcasted_iota(jnp.int32, (tokens, tokens), 0)
             < lax.broadcasted_iota(jnp.int32, (tokens, tokens), 1)).astype(BF)
    before = dot((hits[0] + hits[1]).astype(BF), ahead)
    keys = [ids[k:k + 1, :] * PAD + jnp.sum(hits[k] * before, axis=0, keepdims=True).astype(jnp.int32)
            for k in range(2)]
    r_iota = lax.broadcasted_iota(jnp.int32, (experts * PAD, tokens), 0)
    match = [r_iota == keys[k] for k in range(2)]
    selector = jnp.where(match[0] | match[1], 1.0, 0.0).astype(BF)
    h = hid[...]
    pack[...] = dot(selector, h).astype(BF).reshape(pack.shape)
    lg = lax.dot_general(router_t[...], h, (((1,), (1,)), ((), ())), preferred_element_type=F32)
    lgs[...] = jnp.concatenate([lg, jnp.zeros((experts, 128 - tokens), F32)], axis=1)
    rows = CAP * SHARE
    r_c = lax.broadcasted_iota(jnp.int32, (rows, SHARE * PAD), 0)
    q_c = lax.broadcasted_iota(jnp.int32, (rows, SHARE * PAD), 1)
    group = sum((r_c >= CAP * m).astype(jnp.int32) for m in range(1, SHARE))
    tight = jnp.where(q_c == r_c + (PAD - CAP) * group, 1.0, 0.0).astype(BF)
    q_e = lax.broadcasted_iota(jnp.int32, (SHARE * PAD, rows), 0)
    r_e = lax.broadcasted_iota(jnp.int32, (SHARE * PAD, rows), 1)
    group_e = sum((r_e >= CAP * m).astype(jnp.int32) for m in range(1, SHARE))
    loose = jnp.where(q_e == r_e + (PAD - CAP) * group_e, 1.0, 0.0).astype(BF)

    for n in range(2, len(staged)):
        staged[n].wait()
    channels = x_in.shape[1]
    tiles = channels // 128

    def tiled(ref, values):
        for j in range(tiles):
            ref[:, j, :] = values[:, j * 128:(j + 1) * 128]

    step = jax.nn.softplus(dot(dt_low[...], dt_weight[...]) + dt_bias[...])
    tiled(delta, step)
    tiled(rates, -jnp.exp(a_log[...]))

    mail = Mail(send, recv)
    pl.semaphore_wait(barrier, 16 + 3 + 7 + 1 - 2 * mine.astype(jnp.int32) + jnp.where(ends, 0, 1) + NZ - 1 - z)

    IN1, RT, RS, ACT, YC, YS, ZR = 0, 8, 18, 33, 53, 57, 61
    RET, LG, WG, WD, TAIL, ROW, ZALL, ENTRY = 62, 70, 78, 82, 83, 84, 88, 104

    for near_one, e, to in targets:
        mail.post(pack.at[e], in1.at[c, turn_j], IN1 + 4 * c + turn_j, to, mine if near_one else None)
    mail.post(x_in.at[pl.ds(tokens - 16, 16)], tail, TAIL, (seq + jnp.where(ends, 0, 1), exp), ends)
    own_group = z // 2
    stay = pltpu.make_async_copy(pack.at[own_group], in1.at[c, turn_j], local.at[NX + 1])
    pl.when(mine)(stay.start)
    for q in range(NX):
        mail.post(wg_in.at[:, pl.ds(q * ff, ff)], wg.at[c, q], WG + q, mate)
    mail.post(wd_in, wd.at[c], WD, mate)
    for j in range(1, 8):
        mail.post(lgs, lgr.at[exp], LG + exp, (seq, lax.rem(exp + j, 8)))
    mail.take(tail, TAIL, starts)
    before_rows = tail[...].astype(F32)[8:16]
    padded[0:8] = jnp.where(starts, 0.0, before_rows)
    padded[8:8 + tokens] = x_in[...].astype(F32)
    taps = conv_weight.shape[0]
    convolved = conv_bias[...]
    for k in range(taps):
        convolved = convolved + conv_weight[k:k + 1, :] * padded[9 - taps + k:9 - taps + k + tokens]
    activated = jax.nn.silu(convolved)
    active[...] = activated
    tiled(drive, step * activated)
    states = rates.shape[0]

    def own_step(t, carry):
        d, u = delta[t], drive[t]
        values = []
        for n in range(states):
            f = jnp.exp(d * rates[n])
            factor[t, n] = f
            values.append(f * carry[n] + b_and_c[0, n, t] * u)
        return tuple(values) + (carry[states] + d,)

    blank = jnp.zeros((tiles, 128), F32)
    final_state = lax.fori_loop(0, tokens, own_step, (blank,) * (states + 1))
    for n in range(states + 1):
        rowend[y, n] = final_state[n]
    for i, to_y in enumerate((near[1], near[-1], yfar)):
        mail.post(rowend.at[y], rowend.at[y], ROW + y, at(z, to_y, x, c))

    pl.when(mine)(stay.wait)
    for f, j, to in feeds:
        mail.take(in1.at[f, j], IN1 + 4 * f + j, is_me(f, j))
    feats = hid.shape[1]
    cols = [pl.ds(f * feats, feats) for f in range(2)]
    share = [half, 1 - half]
    for f in range(2):
        rt[0, half, :, cols[f]] = dot(tight, in1[f].reshape(SHARE * PAD, -1)).astype(BF)
    for w in share[:1]:
        mail.post(rt.at[0, w], rt.at[2, w], RT + 4 + w, ypeer[1])
        mail.post(rt.at[0, w], rt.at[1, w], RT + 2 + w, ypeer[-1])
        mail.post(rt.at[0, w], rt.at[0, w], RT + w, zpeer)
    quarter = states // NY

    def along_y():
        for to_y in (near[1], near[-1], yfar):
            mail.take(rowend.at[to_y], ROW + to_y)
        ahead_sum, row_sum = blank, blank
        for other_y in range(NY):
            ahead_sum = jnp.where(y == other_y, row_sum, ahead_sum)
            row_sum = row_sum + rowend[other_y, states]
        for n in range(states):
            total, mine_before = blank, blank
            for other_y in range(NY):
                mine_before = jnp.where(y == other_y, total, mine_before)
                total = jnp.exp(rates[n] * rowend[other_y, states]) * total + rowend[other_y, n]
            state[n] = mine_before
            rowall[n // quarter, n % quarter] = total
        for i in range(NY):
            rowall[i, quarter] = row_sum
        for later in range(1, NZ):
            gone = z + later >= NZ
            mail.post(rowall.at[y], zall.at[z], ZALL + z, at(jnp.where(gone, z, z + later), y, x, c), gone)
        prior[...] = ahead_sum

    def along_z():
        def fold(other_z, carry):
            mail.take(zall.at[other_z], ZALL + other_z)
            decay = zall[other_z, quarter]
            return tuple(jnp.exp(rates[quarter * y + i] * decay) * carry[i] + zall[other_z, i]
                         for i in range(quarter))

        entering = lax.fori_loop(0, z, fold, (blank,) * quarter)
        for i in range(quarter):
            entry[y, i] = entering[i]
        for to_y in (near[1], near[-1], yfar):
            mail.post(entry.at[y], entry.at[y], ENTRY + y, at(z, to_y, x, c))

    def enter():
        for to_y in (near[1], near[-1], yfar):
            mail.take(entry.at[to_y], ENTRY + to_y)
        for n in range(states):
            state[n] = state[n] + jnp.exp(rates[n] * prior[...]) * entry[n // quarter, n % quarter]

    pieces = 4

    def scan_piece(piece):
        def full_step(t, carry):
            u = drive[t]
            values, seen = [], None
            for n in range(states):
                value = factor[t, n] * carry[n] + b_and_c[0, n, t] * u
                values.append(value)
                term = b_and_c[1, n, t] * value
                seen = term if seen is None else seen + term
            reads[t] = seen
            return tuple(values)

        length = tokens // pieces
        done = lax.fori_loop(piece * length, (piece + 1) * length, full_step,
                             tuple(state[n] for n in range(states)))
        for n in range(states):
            state[n] = done[n]

    def finish_mixer():
        for j in range(tiles):
            cols = slice(j * 128, (j + 1) * 128)
            gate = jax.nn.silu(z_gate[:, cols].astype(F32))
            mixed[:, cols] = ((reads[:, j, :] + d_skip[:, cols] * active[:, cols]) * gate).astype(BF)

    for copy in loads:
        copy.wait()
    for q in range(NX):
        mail.take(wg.at[1 - c, q], WG + q)

    def gathered(k, i):
        w = share[i]
        if k == 0:
            mail.take(rt.at[0, w], RT + w)
            mail.post(rt.at[0, w], rt.at[2, w], RT + 4 + w, ypeer[1])
            mail.post(rt.at[0, w], rt.at[1, w], RT + 2 + w, ypeer[-1])
        elif k < 3:
            mail.take(rt.at[k, w], RT + 2 * k + w)
            f = k - 1 if k == 1 else 1
            mail.post(rt.at[k, w, :, cols[f]], rt.at[3, w, :, cols[f]], RT + 6 + 2 * w + f, ypeer[-1 if k == 1 else 1])
        else:
            for f in range(2):
                mail.take(rt.at[3, w, :, cols[f]], RT + 6 + 2 * w + f)

    def take_down():
        mail.take(wd.at[1 - c], WD)

    def part(b, i, q):
        k, w = BATCHES[b][i]
        held = rt.at[k, share[w]]
        return dot(held[:, cols[0]], wg[0, q]) + dot(held[:, cols[1]], wg[1, q])

    way = [1, -1, 1, -1, 1]

    def blocks(b):
        return range(len(BATCHES[b]))

    def span(b):
        return pl.ds(0, len(BATCHES[b]))

    def first(b):
        d, r = way[b], span(b)
        for i in blocks(b):
            sbuf[b, 0, i] = part(b, i, xs[2]).astype(BF)
        mail.post(sbuf.at[b, 0, r], rbuf.at[b, 0, r], RS + 3 * b, xfar if b == DIRECT else xpeer[d])
        if b == DIRECT:
            for slot, way_to in ((1, -d), (2, d)):
                for i in blocks(b):
                    sbuf[b, slot, i] = part(b, i, xs[way_to]).astype(BF)
                mail.post(sbuf.at[b, slot, r], rbuf.at[b, slot, r], RS + 3 * b + slot, xpeer[way_to])
            for i in blocks(b):
                sbuf[b, 3, i] = part(b, i, x).astype(BF)
            return
        for i in blocks(b):
            sbuf[b, 1, i] = part(b, i, xs[-d]).astype(BF)
        mail.post(sbuf.at[b, 1, r], rbuf.at[b, 1, r], RS + 3 * b + 1, xpeer[-d])
        for i in blocks(b):
            sbuf[b, 2, i] = part(b, i, xs[d]).astype(BF)
            sbuf[b, 3, i] = part(b, i, x).astype(BF)

    def second(b):
        d, r = way[b], span(b)
        mail.take(rbuf.at[b, 0, r], RS + 3 * b)
        for i in blocks(b):
            sbuf[b, 4, i] = (sbuf[b, 2, i].astype(F32) + rbuf[b, 0, i].astype(F32)).astype(BF)
        mail.post(sbuf.at[b, 4, r], rbuf.at[b, 2, r], RS + 3 * b + 2, xpeer[d])

    def third(b):
        r = span(b)
        if b == DIRECT:
            mail.take(rbuf.at[b, 0, r], RS + 3 * b)
        mail.take(rbuf.at[b, 1, r], RS + 3 * b + 1)
        mail.take(rbuf.at[b, 2, r], RS + 3 * b + 2)
        for i in blocks(b):
            total = sbuf[b, 3, i].astype(F32) + rbuf[b, 1, i].astype(F32) + rbuf[b, 2, i].astype(F32)
            if b == DIRECT:
                total += rbuf[b, 0, i].astype(F32)
            act[b, x, i] = jax.nn.silu(total).astype(BF)
        for to in (xpeer[1], xpeer[-1]) + ((xfar,) if b == DIRECT else ()):
            mail.post(act.at[b, x, r], act.at[b, x, r], ACT + 4 * b + x, to)

    def fourth(b):
        d, r = way[b], span(b)
        mail.take(act.at[b, xs[-d], r], ACT + 4 * b + xs[-d])
        mail.post(act.at[b, xs[-d], r], act.at[b, xs[-d], r], ACT + 4 * b + xs[-d], xpeer[d])

    def down(b):
        d, r = way[b], span(b)
        mail.take(act.at[b, xs[d], r], ACT + 4 * b + xs[d])
        if b == DIRECT:
            mail.take(act.at[b, xs[-d], r], ACT + 4 * b + xs[-d])
        mail.take(act.at[b, xs[2], r], ACT + 4 * b + xs[2])
        for i in blocks(b):
            k, w = BATCHES[b][i]
            for f in range(2):
                total = dot(act[b, 0, i], wd[f, 0:ff])
                for q in range(1, NX):
                    total += dot(act[b, q, i], wd[f, q * ff:(q + 1) * ff])
                prod[k, share[w], :, cols[f]] = total.astype(BF)

    def far(i):
        w = share[i]
        for f, d in ((0, 1), (1, -1)):
            mail.post(prod.at[3, w, :, cols[f]], yc.at[w, f], YC + 2 * w + f, ypeer[d])

    def combine(i):
        w = share[i]
        for f, d in ((0, 1), (1, -1)):
            mail.take(yc.at[w, f], YC + 2 * w + f)
            zs[w, f, :, cols[f]] = (prod[1 + f, w, :, cols[f]].astype(F32) + yc[w, f].astype(F32)).astype(BF)
            zs[w, f, :, cols[1 - f]] = prod[1 + f, w, :, cols[1 - f]]
            mail.post(zs.at[w, f], ys.at[w, f], YS + 2 * w + f, ypeer[d])

    steps = [
        (first, 0), (gathered, 1, 0), (gathered, 2, 0), (gathered, 0, 1), (first, 1), (second, 0), (gathered, 3, 0),
        (third, 0), (second, 1), (gathered, 1, 1), (gathered, 2, 1), (fourth, 0), (gathered, 3, 1), (first, 2),
        (third, 1), (first, 3), (along_y,), (second, 2), (fourth, 1), (take_down,), (down, 0), (first, 4), (second, 3), (third, 2),
        (down, 1), (fourth, 2), (third, 3), (down, 2), (far, 0), (far, 1), (third, 4),
        (fourth, 3), (combine, 0), (down, 3), (combine, 1), (down, 4)]
    for step_of, *which in steps:
        step_of(*which)

    def over_y(i):
        w = share[i]
        for f in range(2):
            mail.take(ys.at[w, f], YS + 2 * w + f)
        return prod[0, w].astype(F32) + ys[w, 0].astype(F32) + ys[w, 1].astype(F32)

    passed, kept = over_y(1), None
    for f in range(2):
        zb[f] = passed[:, f * feats:(f + 1) * feats].astype(BF)
        mail.post(zb.at[f], zr.at[f], ZR + 47 * f, zpeer)
    along_z()
    kept = over_y(0)
    for f in range(2):
        mail.take(zr.at[f], ZR + 47 * f)
        whole = (kept[:, f * feats:(f + 1) * feats] + zr[f].astype(F32)).astype(BF)
        back[f] = dot(loose, whole).astype(BF).reshape(back.shape[1:])
        for g, j, to in feeds:
            if g == f:
                mail.post(back.at[f, j], ret.at[own_group], RET + own_group, to, is_me(f, j))
    last = pltpu.make_async_copy(back.at[c, turn_j], ret.at[own_group], local.at[NX + 2])
    pl.when(mine)(last.start)

    enter()
    for piece in range(pieces):
        scan_piece(piece)
    finish_mixer()
    for j in range(1, 8):
        q = lax.rem(exp + j, 8)
        mail.take(lgr.at[q], LG + q)
    lgr[exp] = lgs[...]
    logits = lgr[0]
    for q in range(1, 8):
        logits += lgr[q]
    logits = logits[:, :tokens]
    picked = [jnp.sum(hits[k] * logits, axis=0, keepdims=True) for k in range(2)]
    gates = [jax.nn.sigmoid(picked[0] - picked[1]), jax.nn.sigmoid(picked[1] - picked[0])]
    blend = jnp.where(match[0], gates[0], 0.0) + jnp.where(match[1], gates[1], 0.0)
    upper = blend.astype(BF)
    lower = (blend - upper.astype(F32)).astype(BF)

    pl.when(mine)(last.wait)
    for near_one, e, to in targets:
        mail.take(ret.at[e], RET + e, mine if near_one else None)
    rows_in = ret[...].reshape(experts * PAD, -1)
    turn = (((0,), (0,)), ((), ()))
    out[...] = (lax.dot_general(upper, rows_in, turn, preferred_element_type=F32)
                + lax.dot_general(lower, rows_in, turn, preferred_element_type=F32)).astype(BF)
    mail.finish()


def deliver(a, b, a_out, b_out, a_held, b_held, sems):
    ways = ((a, a_held, a_out), (b, b_held, b_out))
    for leg in range(2):
        copies = [pltpu.make_async_copy(way[leg], way[leg + 1], sems.at[n]) for n, way in enumerate(ways)]
        for copy in copies:
            copy.start()
        for copy in copies:
            copy.wait()


def local(x_in, z_gate, dt_low, dt_weight, dt_bias, a_log, conv_weight, conv_bias, d_skip, b_and_c,
          hidden, router, expert_ids, w_gate, w_down):
    tokens, feats = hidden.shape
    channels, states = x_in.shape[1], a_log.shape[0]
    tiles, quarter = channels // 128, states // NY
    rows, ff = CAP * SHARE, w_gate.shape[1] // NX
    vm = pl.BlockSpec(memory_space=pltpu.VMEM)
    hbm = pl.BlockSpec(memory_space=pl.ANY)
    sm = pl.BlockSpec(memory_space=pltpu.SMEM)

    results_shape = (jax.ShapeDtypeStruct((tokens, channels), BF), jax.ShapeDtypeStruct((tokens, feats), BF))

    def row(a):
        return a.reshape(1, channels)

    results = pl.pallas_call(
        layer_kernel,
        out_shape=results_shape,
        in_specs=[hbm] * 9 + [sm] + [hbm] * 2 + [vm] + [hbm] * 2,
        out_specs=(vm, vm),
        scratch_shapes=[
            pltpu.VMEM((2, NX, feats, ff), BF),
            pltpu.VMEM((2, NX * ff, feats), BF),
            pltpu.VMEM((8, PAD, feats), BF),
            pltpu.VMEM((2, SHARE, PAD, feats), BF),
            pltpu.VMEM((4, 2, rows, 2 * feats), BF),
            pltpu.VMEM((len(BATCHES), 5, 2, rows, ff), BF),
            pltpu.VMEM((len(BATCHES), 3, 2, rows, ff), BF),
            pltpu.VMEM((len(BATCHES), NX, 2, rows, ff), BF),
            pltpu.VMEM((4, 2, rows, 2 * feats), BF),
            pltpu.VMEM((2, 2, rows, 2 * feats), BF),
            pltpu.VMEM((2, 2, rows, feats), BF),
            pltpu.VMEM((2, 2, rows, 2 * feats), BF),
            pltpu.VMEM((2, rows, feats), BF),
            pltpu.VMEM((2, SHARE, PAD, feats), BF),
            pltpu.VMEM((8, PAD, feats), BF),
            pltpu.VMEM((8, 128), F32),
            pltpu.VMEM((8, 8, 128), F32),
            pltpu.VMEM((2, rows, feats), BF),
            pltpu.VMEM((tiles, 128), F32),
            pltpu.VMEM((16, channels), BF),
            pltpu.VMEM((8 + tokens, channels), F32),
            pltpu.VMEM((tokens, channels), F32),
            pltpu.VMEM((tokens, tiles, 128), F32),
            pltpu.VMEM((tokens, tiles, 128), F32),
            pltpu.VMEM((states, tiles, 128), F32),
            pltpu.VMEM((tokens, states, tiles, 128), F32),
            pltpu.VMEM((states, tiles, 128), F32),
            pltpu.VMEM((NY, states + 1, tiles, 128), F32),
            pltpu.VMEM((NY, quarter + 1, tiles, 128), F32),
            pltpu.VMEM((NZ, quarter + 1, tiles, 128), F32),
            pltpu.VMEM((NY, quarter, tiles, 128), F32),
            pltpu.VMEM((tokens, tiles, 128), F32),
            pltpu.SemaphoreType.DMA((128,)),
            pltpu.SemaphoreType.DMA((128,)),
            pltpu.SemaphoreType.DMA((8,)),
            pltpu.SemaphoreType.DMA((16,)),
            pltpu.VMEM((tokens, channels), BF),
            pltpu.VMEM((tokens, channels), BF),
            pltpu.VMEM(dt_low.shape, BF),
            pltpu.VMEM(dt_weight.shape, BF),
            pltpu.VMEM((1, channels), F32),
            pltpu.VMEM(a_log.shape, F32),
            pltpu.VMEM(conv_weight.shape, F32),
            pltpu.VMEM((1, channels), F32),
            pltpu.VMEM((1, channels), F32),
            pltpu.VMEM(hidden.shape, BF),
            pltpu.VMEM(router.shape[::-1], BF),
        ],
        compiler_params=pltpu.CompilerParams(collective_id=0, has_side_effects=True,
                                             vmem_limit_bytes=60 * 1024 * 1024),
        name="layer",
    )(x_in, z_gate, dt_low, dt_weight, row(dt_bias), a_log, conv_weight, row(conv_bias), row(d_skip), b_and_c,
      hidden, router.T, expert_ids.T, w_gate, w_down)
    return pl.pallas_call(deliver, out_shape=results_shape, in_specs=[hbm] * 2, out_specs=(hbm, hbm),
                          scratch_shapes=[pltpu.VMEM((tokens, channels), BF), pltpu.VMEM((tokens, feats), BF),
                                          pltpu.SemaphoreType.DMA((2,))], name="deliver")(*results)


def solution(mesh):
    return jax.shard_map(
        local,
        mesh=mesh,
        in_specs=(
            P("seq", "exp"),
            P("seq", "exp"),
            P("seq", None),
            P(None, "exp"),
            P("exp"),
            P(None, "exp"),
            P(None, "exp"),
            P("exp"),
            P("exp"),
            P(None, None, "seq"),
            P("seq", "exp"),
            P("exp", None),
            P("seq", None),
            P("exp", "seq"),
            P("seq", "exp"),
        ),
        out_specs=(P("seq", "exp"), P("seq", "exp")),
        check_vma=False,
    )
```
